128 devices in a mesh: dp: 16 (over x, z_hi, core), tensor: 8 (over z_lo, y).
Axes of the slice: x: 4, y: 4, z: 4 (z_hi: 2, z_lo: 2; z = z_hi * 2 + z_lo), core: 2. Of those that a mesh axis runs over, the one named last changes fastest.
Arguments:
- gate_pre: bfloat16 [16384, 7168], P('dp', 'tensor'), may hold values from -6 to 6
- up_pre: bfloat16 [16384, 7168], P('dp', 'tensor'), may hold values from -6 to 6
- down_weight: bfloat16 [7168, 4096], P('tensor'), may hold values from -0.0625 to 0.0625
- grad_out: bfloat16 [16384, 4096], P(('dp', 'tensor')), may hold values from -24 to 24
Outputs:
- ffn_out: bfloat16 [16384, 4096], P(('dp', 'tensor'))
- grad_gate: bfloat16 [16384, 7168], P('dp', 'tensor')
- grad_up: bfloat16 [16384, 7168], P('dp', 'tensor')
- grad_down: float32 [7168, 4096], P('tensor', 'dp')
The draws below stay inside these ranges and needn't reach their ends.
All inputs are finite; a program needn't handle non-finite values.
Results may differ from the reference program's by a relative error of at most 0.017.
Values may be sent and summed in bfloat16 or wider, within the bound.
A program may use at most 128 MiB of HBM per device.

```python
import math
import jax
import jax.numpy as jnp
from jax import lax

D = 4096
FF_DEV = 896
TOK_DEV = 128
FF = 7168
TOKENS = 16384
N_DP = 16
N_TENSOR = 8


def with_spikes(array, own_key, source, target, shards_of, factor):
    def block_of(dim):
        return (jnp.arange(array.shape[dim]) // (array.shape[dim] // shards_of)).reshape((-1,) + (1,) * (array.ndim - 1 - dim))

    one_side = jax.random.permutation(own_key, shards_of)[block_of(target)]
    far = (block_of(target) + shards_of // 2) % shards_of
    return jnp.where((block_of(source) == one_side) | (block_of(source) == far), factor * array, array)


def shard_levels(key, shape, split, least, high):
    factor_of, own = 1.0, jax.random.fold_in(key, 6)
    for position, blocks in split:
        heights = jnp.exp(jax.random.uniform(jax.random.fold_in(own, position), (blocks,), jnp.float32, least / len(split), high / len(split)))
        factor_of = factor_of * jnp.repeat(heights, shape[position] // blocks).reshape([-1 if axis == position else 1 for axis in range(len(shape))])
    return factor_of


def gaussian(stream_key, dims, scale, bound, split=(), dtype=jnp.bfloat16):
    drawn = scale * jax.random.normal(stream_key, dims, jnp.float32)
    if split:
        drawn = drawn * shard_levels(stream_key, dims, split, -0.22, 0.18)
    return jnp.clip(drawn, -bound, bound).astype(dtype)


def heavy_noise(own_key, shape, width, bound, cuts, heavy, dtype=jnp.bfloat16):
    result = width * jax.random.normal(own_key, shape, jnp.float32)
    if cuts:
        result = result * shard_levels(own_key, shape, cuts, -0.22, 0.18)
    return jnp.clip(with_spikes(result, jax.random.fold_in(own_key, 3), *heavy), -bound, bound).astype(dtype)


def setup_inputs(seed: int = 0) -> dict:
    key_of = jax.random.split(jax.random.key(seed), 5)
    gate_pre = gaussian(key_of[0], (TOKENS, FF), 1.0, 6.0, ((0, 16), (1, 8)))
    up_pre = gaussian(key_of[1], (TOKENS, FF), 1.0, 6.0, ((0, 16), (1, 8)))
    down_weight = gaussian(key_of[2], (FF, D), FF ** -0.5, 0.0625, ((0, 8),))
    grad_out = heavy_noise(key_of[3], (TOKENS, D), 1.0, 24.0, ((0, 128),), (0, 1, 128, 5.5))
    return dict(gate_pre=gate_pre, up_pre=up_pre, down_weight=down_weight, grad_out=grad_out)


def reference(gate_pre, up_pre, down_weight, grad_out):
    gate_val = gate_pre.astype(jnp.float32)
    up_val = up_pre.astype(jnp.float32)
    sigmoid_gate = jax.nn.sigmoid(gate_val)
    activated = gate_val * sigmoid_gate
    hidden = (activated * up_val).astype(jnp.bfloat16)
    hidden_blocks = hidden.reshape(TOKENS, N_TENSOR, FF_DEV).transpose(1, 0, 2)
    weight_blocks = down_weight.reshape(N_TENSOR, FF_DEV, D)

    def add_partial(total, pair):
        block_rows, block_weight = pair
        partial_value = jnp.dot(block_rows, block_weight, preferred_element_type=jnp.float32)
        return (total + partial_value.astype(jnp.bfloat16).astype(jnp.float32), None)
    output_sum, _ = lax.scan(add_partial, jnp.zeros((TOKENS, D), jnp.float32), (hidden_blocks, weight_blocks))
    ffn_out = output_sum.astype(jnp.bfloat16)
    hidden_grad = jnp.dot(grad_out, down_weight.T, preferred_element_type=jnp.float32)
    grad_gate = (hidden_grad * up_val * sigmoid_gate * (1.0 + gate_val * (1.0 - sigmoid_gate))).astype(jnp.bfloat16)
    grad_up = (hidden_grad * activated).astype(jnp.bfloat16)
    grad_scale = 1.0 / math.sqrt(TOKENS)
    replica_rows = TOK_DEV * N_TENSOR
    hidden_reps = hidden.reshape(N_DP, replica_rows, FF)
    cotangent_reps = grad_out.reshape(N_DP, replica_rows, D)

    def add_replica(total, pair):
        rep_hidden, rep_cotangent = pair
        product = jnp.dot(rep_hidden.T, rep_cotangent, preferred_element_type=jnp.float32) * grad_scale
        return (total + product.astype(jnp.bfloat16).astype(jnp.float32), None)
    grad_down, _ = lax.scan(add_replica, jnp.zeros((FF, D), jnp.float32), (hidden_reps, cotangent_reps))
    return (ffn_out, grad_gate, grad_up, grad_down)
```

```python
import functools
import math

import jax
import jax.numpy as jnp
from jax import lax
from jax.experimental import pallas as pl
from jax.experimental.pallas import tpu as pltpu
from jax.sharding import PartitionSpec as P

MESH = pl.DeviceIdType.MESH
F32 = jnp.float32
BF16 = jnp.bfloat16

STEPS = 8
WIDTH = 512
HALF = 256
ROWS = 128
RA = 80
RB = ROWS - RA
FF = 896

LOOKAHEAD = 3
OFF = dict(A1=0, A2=1, A3=2, D1=3, R0=0, R1=1, R2=4, R3=5, R4=6, E=10, D2A=10, D2B=12)
ITERS = 14


def add_rows(dst, srcs, rows):
    def step(t, carry):
        sl = pl.ds(pl.multiple_of(t * 16, 16), 16)
        total = dst[sl, :].astype(F32)
        for src in srcs:
            total += src[sl, :].astype(F32)
        dst[sl, :] = total.astype(dst.dtype)
        return carry

    lax.fori_loop(0, rows // 16, step, 0)


def kernel(
    scale,
    gate_hbm, up_hbm, w_hbm, g_hbm,
    f_out, gg_out, gu_out, gd_out,
    gate_v, up_v, w_v, h_v, ht_v, gb, p, hg,
    rz1, rho, rhw, rfo, rfw, rz2,
    cs, ck, cr, xr, zs, zr, gd_v,
    ag_s, ag_r, rs_s, rs_r, c_s, c_r, x_s, x_r, zh_s, zh_r,
    ld_g, ld_w, ld_a, st_f, st_e, st_d,
):
    dp = lax.axis_index("dp")
    te = lax.axis_index("tensor")
    x, zh, core = dp // 4, (dp // 2) % 2, dp % 2
    z, y = te // 4, te % 4
    yp, ym, y2 = (y + 1) % 4, (y + 3) % 4, (y + 2) % 4
    zo = 1 - z
    own, other = z * 4, zo * 4
    to_yp, to_ym, to_z = (dp, own + yp), (dp, own + ym), (dp, other + y)
    to_core = (x * 4 + zh * 2 + (1 - core), te)
    to_zh = (x * 4 + (1 - zh) * 2 + core, te)

    def to_x(d):
        return (((x + d) % 4) * 4 + zh * 2 + core, te)

    def column(s):
        j = 2 * ((x + 1 + s // 2) % 4) + (s + 1 + zh) % 2
        return pl.ds(pl.multiple_of(j * WIDTH, WIDTH), WIDTH)

    def load_g(s):
        return pltpu.make_async_copy(g_hbm.at[:, column(s)], gb.at[s, te], ld_g.at[s])

    def load_w(s):
        return pltpu.make_async_copy(w_hbm.at[:, column(s)], w_v.at[s], ld_w.at[s])

    load_gate = pltpu.make_async_copy(gate_hbm, gate_v, ld_a.at[0])
    load_up = pltpu.make_async_copy(up_hbm, up_v, ld_a.at[1])

    def each(n, f):
        def step(s, carry):
            f(s)
            return carry

        lax.fori_loop(0, n, step, 0)

    each(STEPS, lambda s: load_g(s).start())
    load_gate.start()
    load_up.start()
    each(STEPS, lambda s: load_w(s).start())

    barrier = pltpu.get_barrier_semaphore()
    for device in (to_yp, to_ym, to_z, to_core, to_zh, to_x(1), to_x(2), to_x(3)):
        pl.semaphore_signal(barrier, inc=1, device_id=device, device_id_type=MESH)
    pl.semaphore_wait(barrier, 8)

    def remote(src, dst, send, recv, device):
        return pltpu.make_async_remote_copy(
            src_ref=src, dst_ref=dst, send_sem=send, recv_sem=recv,
            device_id=device, device_id_type=MESH,
        )

    ROW_ALL, ROW_A, ROW_B = pl.ds(0, ROWS), pl.ds(0, RA), pl.ds(RA, RB)
    COL_ALL, COL_0, COL_1 = pl.ds(0, WIDTH), pl.ds(0, HALF), pl.ds(HALF, HALF)

    gather = (
        (own + y, other + y, ROW_ALL, COL_ALL, to_z),
        (own + y, own + ym, ROW_ALL, COL_ALL, to_yp),
        (own + y, own + yp, ROW_ALL, COL_ALL, to_ym),
        (other + y, other + ym, ROW_A, COL_ALL, to_yp),
        (other + y, other + yp, ROW_A, COL_ALL, to_ym),
        (own + yp, own + y2, ROW_ALL, COL_0, to_ym),
        (own + ym, own + y2, ROW_ALL, COL_1, to_yp),
        (own + yp, other + yp, ROW_B, COL_ALL, to_z),
        (own + ym, other + ym, ROW_B, COL_ALL, to_z),
        (other + yp, other + y2, ROW_A, COL_0, to_ym),
        (other + ym, other + y2, ROW_A, COL_1, to_yp),
        (own + y2, other + y2, ROW_B, COL_0, to_z),
        (own + y2, other + y2, ROW_B, COL_1, to_z),
    )

    def ag(k, s, arriving=False):
        leaves, arrives, rows, cols, device = gather[k]
        ref = gb.at[s, arrives if arriving else leaves, rows, cols]
        return remote(ref, ref, ag_s.at[k, s], ag_r.at[k, s], device)

    def ag_send(k, s):
        ag(k, s).start()

    def ag_wait(k, s):
        ag(k, s, True).wait_recv()

    reduction = (
        (other + yp, ROW_B, COL_ALL, rz1, 0, to_z),
        (other + ym, ROW_B, COL_ALL, rz1, 1, to_z),
        (other + y2, ROW_B, COL_ALL, rz1, 2, to_z),
        (other + y2, ROW_A, COL_0, rho, 0, to_yp),
        (other + y2, ROW_A, COL_1, rho, 1, to_ym),
        (own + y2, ROW_ALL, COL_0, rhw, 0, to_yp),
        (own + y2, ROW_ALL, COL_1, rhw, 1, to_ym),
        (other + yp, ROW_A, COL_ALL, rfo, 0, to_yp),
        (other + ym, ROW_A, COL_ALL, rfo, 1, to_ym),
        (own + yp, ROW_ALL, COL_ALL, rfw, 0, to_yp),
        (own + ym, ROW_ALL, COL_ALL, rfw, 1, to_ym),
        (other + y, ROW_ALL, COL_ALL, rz2, 0, to_z),
    )

    def rs(k, s):
        slot, rows, cols, land, index, device = reduction[k]
        return remote(p.at[s, slot, rows, cols], land.at[s, index], rs_s.at[k, s], rs_r.at[k, s], device)

    def rs_send(k, s):
        rs(k, s).start()

    def rs_wait(k, s):
        rs(k, s).wait_recv()

    def core_copy(s):
        return remote(cs.at[s], cr.at[s], c_s.at[s], c_r.at[s], to_core)

    def x_copy(s):
        return remote(ck.at[s], xr.at[s], x_s.at[s], x_r.at[s], to_x(1 + s // 2))

    zh_copy = remote(zs, zr, zh_s, zh_r, to_zh)

    def a0(s):
        load_g(s).wait()
        for k in (1, 2, 0):
            ag_send(k, s)

    def a1(s):
        ag_wait(0, s)
        ag_send(3, s)
        ag_send(4, s)
        ag_wait(2, s)
        ag_send(5, s)
        ag_send(7, s)
        ag_wait(1, s)
        ag_send(6, s)
        ag_send(8, s)

    def a2(s):
        ag_wait(4, s)
        ag_send(9, s)
        ag_wait(3, s)
        ag_send(10, s)
        ag_wait(5, s)
        ag_send(11, s)
        ag_wait(6, s)
        ag_send(12, s)

    def a3(s):
        for k in range(7, 13):
            ag_wait(k, s)

        def weight_half(side, dst):
            cols = pl.ds(pl.multiple_of(side * HALF, HALF), HALF)

            def tile(t, carry):
                rows = pl.ds(pl.multiple_of(t * 448, 64), 448)
                block = gb[s, :, :, cols].reshape(8 * ROWS, HALF)
                product = jnp.dot(ht_v[rows, :], block, preferred_element_type=F32)
                dst[s, rows, :] = (product * scale).astype(BF16)
                return carry

            lax.fori_loop(0, 2, tile, 0)

        weight_half(1 - core, cs)
        core_copy(s).start()
        weight_half(core, ck)

        def tile(t, carry):
            rows = pl.ds(pl.multiple_of(t * 512, 512), 512)
            block = gb[s, pl.ds(t * 4, 4)].reshape(512, WIDTH)
            product = lax.dot_general(
                block, w_v[s], (((1,), (1,)), ((), ())), preferred_element_type=F32
            )

            @pl.when(s == 0)
            def _():
                hg[rows, :] = product

            @pl.when(s > 0)
            def _():
                hg[rows, :] += product

            return carry

        lax.fori_loop(0, 2, tile, 0)

    def d1(s):
        core_copy(s).wait_recv()
        add_rows(ck.at[s], [cr.at[s]], FF)

        @pl.when(s < 6)
        def _():
            x_copy(s).start()

    def d2a():
        for k in (0, 2, 4):
            x_copy(k).wait_recv()

        def tile(t, carry):
            sl = pl.ds(pl.multiple_of(t * 16, 16), 16)
            total = ck[6, sl, :].astype(F32)
            for k in (0, 2, 4):
                total += xr[k, sl, :].astype(F32)
            zs[sl, :] = total.astype(BF16)
            return carry

        lax.fori_loop(0, FF // 16, tile, 0)
        zh_copy.start()

    save_d = pltpu.make_async_copy(gd_v, gd_out, st_d)

    def d2b():
        for k in (1, 3, 5):
            x_copy(k).wait_recv()
        zh_copy.wait_recv()

        def tile(t, carry):
            sl = pl.ds(pl.multiple_of(t * 16, 16), 16)
            total = ck[7, sl, :].astype(F32) + zr[sl, :].astype(F32)
            for k in (1, 3, 5):
                total += xr[k, sl, :].astype(F32)
            gd_v[sl, :] = total
            return carry

        lax.fori_loop(0, FF // 16, tile, 0)
        save_d.start()

    def r0(s):
        load_w(s).wait()

        def tile(t, carry):
            rows = pl.ds(pl.multiple_of(t * 512, 512), 512)
            product = jnp.dot(h_v[rows, :], w_v[s], preferred_element_type=F32)
            p[s, pl.ds(t * 4, 4)] = product.astype(BF16).reshape(4, ROWS, WIDTH)
            return carry

        lax.fori_loop(0, 2, tile, 0)
        for k in (0, 1, 2, 3, 4):
            rs_send(k, s)

    def r1(s):
        for k, slot in ((2, own + y2), (0, own + yp), (1, own + ym)):
            rs_wait(k, s)
            add_rows(p.at[s, slot, ROW_B, :], [rz1.at[s, k]], RB)
            if k == 2:
                rs_send(5, s)
                rs_send(6, s)

    def r2(s):
        rs_wait(3, s)
        add_rows(p.at[s, other + yp, ROW_A, COL_0], [rho.at[s, 0]], RA)
        rs_send(7, s)
        rs_wait(4, s)
        add_rows(p.at[s, other + ym, ROW_A, COL_1], [rho.at[s, 1]], RA)
        rs_send(8, s)
        rs_wait(5, s)
        add_rows(p.at[s, own + yp, ROW_ALL, COL_0], [rhw.at[s, 0]], ROWS)
        rs_send(9, s)
        rs_wait(6, s)
        add_rows(p.at[s, own + ym, ROW_ALL, COL_1], [rhw.at[s, 1]], ROWS)
        rs_send(10, s)

    def r3(s):
        rs_wait(7, s)
        rs_wait(8, s)
        add_rows(p.at[s, other + y, ROW_A, :], [rfo.at[s, 0], rfo.at[s, 1]], RA)
        rs_send(11, s)

    def save_f(s):
        return pltpu.make_async_copy(p.at[s, te], f_out.at[:, column(s)], st_f.at[s])

    def r4(s):
        for k in (9, 10, 11):
            rs_wait(k, s)
        add_rows(p.at[s, te], [rfw.at[s, 0], rfw.at[s, 1], rz2.at[s, 0]], ROWS)
        save_f(s).start()

    def save_e(e, which):
        rows = pl.ds(pl.multiple_of(e * 256, 256), 256)
        src, dst = ((gate_v, gg_out), (up_v, gu_out))[which]
        return pltpu.make_async_copy(src.at[rows, :], dst.at[rows, :], st_e.at[which, e])

    def e0(e):
        def tile(t, carry):
            sl = pl.ds(pl.multiple_of(e * 256 + t * 16, 16), 16)
            g = gate_v[sl, :].astype(F32)
            u = up_v[sl, :].astype(F32)
            grad = hg[sl, :]
            s = jax.nn.sigmoid(g)
            gate_v[sl, :] = (grad * u * s * (1.0 + g * (1.0 - s))).astype(BF16)
            up_v[sl, :] = (grad * (g * s)).astype(BF16)
            return carry

        lax.fori_loop(0, 16, tile, 0)
        save_e(e, 0).start()
        save_e(e, 1).start()

    each(LOOKAHEAD, a0)
    load_gate.wait()
    load_up.wait()

    def hidden_tile(t, carry):
        sl = pl.ds(pl.multiple_of(t * 16, 16), 16)
        g = gate_v[sl, :].astype(F32)
        u = up_v[sl, :].astype(F32)
        h_v[sl, :] = (g * jax.nn.sigmoid(g) * u).astype(BF16)
        return carry

    lax.fori_loop(0, 64, hidden_tile, 0)

    def transpose_tile(t, carry):
        sl = pl.ds(pl.multiple_of(t * 128, 128), 128)
        ht_v[:, sl] = h_v[sl, :].T
        return carry

    lax.fori_loop(0, 8, transpose_tile, 0)

    def iteration(i, carry):
        def stage(name, f, count=STEPS):
            s = i - OFF[name]

            @pl.when((s >= 0) & (s < count))
            def _():
                f(s)

        @pl.when(i + LOOKAHEAD < STEPS)
        def _():
            a0(i + LOOKAHEAD)

        stage("A1", a1)
        stage("R0", r0)
        stage("A2", a2)
        stage("R1", r1)
        stage("R2", r2)
        stage("R3", r3)
        stage("A3", a3)
        stage("D1", d1)
        stage("D2A", lambda s: d2a(), 1)
        stage("R4", r4)
        stage("E", e0, 4)
        stage("D2B", lambda s: d2b(), 1)
        return carry

    lax.fori_loop(0, ITERS, iteration, 0)

    def finish(s):
        for k in range(13):
            ag(k, s).wait_send()
        for k in range(12):
            rs(k, s).wait_send()
        core_copy(s).wait_send()
        save_f(s).wait()

    each(STEPS, finish)
    each(6, lambda s: x_copy(s).wait_send())
    zh_copy.wait_send()

    def finish_e(e):
        save_e(e, 0).wait()
        save_e(e, 1).wait()

    each(4, finish_e)
    save_d.wait()


def body(gate_pre, up_pre, down_weight, grad_out):
    replica_rows, ff = gate_pre.shape
    rows, width = grad_out.shape
    scale = 1.0 / math.sqrt(replica_rows * lax.axis_size("dp"))
    vmem, dma = pltpu.VMEM, pltpu.SemaphoreType.DMA
    anywhere = pl.BlockSpec(memory_space=pl.ANY)
    return pl.pallas_call(
        functools.partial(kernel, scale),
        out_shape=(
            jax.ShapeDtypeStruct((rows, width), BF16),
            jax.ShapeDtypeStruct((replica_rows, ff), BF16),
            jax.ShapeDtypeStruct((replica_rows, ff), BF16),
            jax.ShapeDtypeStruct((ff, width // 16), F32),
        ),
        in_specs=[anywhere] * 4,
        out_specs=[anywhere] * 4,
        scratch_shapes=[
            vmem((replica_rows, ff), BF16),
            vmem((replica_rows, ff), BF16),
            vmem((STEPS, ff, WIDTH), BF16),
            vmem((replica_rows, ff), BF16),
            vmem((ff, replica_rows), BF16),
            vmem((STEPS, 8, ROWS, WIDTH), BF16),
            vmem((STEPS, 8, ROWS, WIDTH), BF16),
            vmem((replica_rows, ff), F32),
            vmem((STEPS, 3, RB, WIDTH), BF16),
            vmem((STEPS, 2, RA, HALF), BF16),
            vmem((STEPS, 2, ROWS, HALF), BF16),
            vmem((STEPS, 2, RA, WIDTH), BF16),
            vmem((STEPS, 2, ROWS, WIDTH), BF16),
            vmem((STEPS, 1, ROWS, WIDTH), BF16),
            vmem((STEPS, ff, HALF), BF16),
            vmem((STEPS, ff, HALF), BF16),
            vmem((STEPS, ff, HALF), BF16),
            vmem((6, ff, HALF), BF16),
            vmem((ff, HALF), BF16),
            vmem((ff, HALF), BF16),
            vmem((ff, HALF), F32),
            dma((13, STEPS)), dma((13, STEPS)),
            dma((12, STEPS)), dma((12, STEPS)),
            dma((STEPS,)), dma((STEPS,)),
            dma((6,)), dma((6,)),
            dma, dma,
            dma((STEPS,)), dma((STEPS,)), dma((2,)),
            dma((STEPS,)), dma((2, 4)), dma,
        ],
        compiler_params=pltpu.CompilerParams(
            collective_id=0, has_side_effects=True, vmem_limit_bytes=60 * 1024 * 1024
        ),
        cost_estimate=pl.CostEstimate(
            flops=6 * replica_rows * ff * width, bytes_accessed=20_000_000, transcendentals=2_000_000
        ),
    )(gate_pre, up_pre, down_weight, grad_out)


def solution(mesh):
    return jax.shard_map(
        body,
        mesh=mesh,
        in_specs=(
            P("dp", "tensor"),
            P("dp", "tensor"),
            P("tensor", None),
            P(("dp", "tensor"), None),
        ),
        out_specs=(
            P(("dp", "tensor"), None),
            P("dp", "tensor"),
            P("dp", "tensor"),
            P("tensor", "dp"),
        ),
        check_vma=False,
    )
```

```python
import functools
import math

import jax
import jax.numpy as jnp
from jax import lax
from jax.experimental import pallas as pl
from jax.experimental.pallas import tpu as pltpu
from jax.sharding import PartitionSpec as P

MESH = pl.DeviceIdType.MESH
F32 = jnp.float32
BF16 = jnp.bfloat16

STEPS = 8
WIDTH = 512
HALF = 256
ROWS = 128
RA = 48
RB = 32
RC = 48
RAB = RA + RB
FF = 896

LOOKAHEAD = 3
OFF = dict(A1=0, HX=1, A2=1, A3=2, D1=3, R0=1, R1=2, R2=4, R3=5, R4=6, GX=9, GR=11, E=10, D2A=10, D2B=12)
ITERS = 14


def add_rows(dst, srcs, rows):
    def step(t, carry):
        sl = pl.ds(pl.multiple_of(t * 16, 16), 16)
        total = dst[sl, :].astype(F32)
        for src in srcs:
            total += src[sl, :].astype(F32)
        dst[sl, :] = total.astype(dst.dtype)
        return carry

    lax.fori_loop(0, rows // 16, step, 0)


def kernel(
    scale,
    gate_hbm, up_hbm, w_hbm, g_hbm,
    f_out, gg_out, gu_out, gd_out,
    gate_v, up_v, w_v, h_v, ht_v, gb, p, hg,
    rz1, rho, rhw, rfo, rfw, rz2,
    hx, gs, gr,
    cs, ck, cr, xr, zs, zr, gd_v,
    ag_s, ag_r, rs_s, rs_r, c_s, c_r, x_s, x_r, zh_s, zh_r, sw_s, sw_r,
    ld_g, ld_w, ld_a, st_f, st_e, st_d,
):
    dp = lax.axis_index("dp")
    te = lax.axis_index("tensor")
    x, zh, core = dp // 4, (dp // 2) % 2, dp % 2
    z, y = te // 4, te % 4
    yp, ym, y2 = (y + 1) % 4, (y + 3) % 4, (y + 2) % 4
    zo = 1 - z
    own, other = z * 4, zo * 4
    to_yp, to_ym, to_z = (dp, own + yp), (dp, own + ym), (dp, other + y)
    to_core = (x * 4 + zh * 2 + (1 - core), te)
    to_zh = (x * 4 + (1 - zh) * 2 + core, te)
    to_zc = (x * 4 + (1 - zh) * 2 + core, other + y)

    def to_x(d):
        return (((x + d) % 4) * 4 + zh * 2 + core, te)

    def column(s):
        j = 2 * ((x + 1 + s // 2) % 4) + s % 2
        return pl.ds(pl.multiple_of(j * WIDTH, WIDTH), WIDTH)

    def load_g(s):
        return pltpu.make_async_copy(g_hbm.at[:, column(s)], gb.at[s, te], ld_g.at[s])

    def load_w(s):
        return pltpu.make_async_copy(w_hbm.at[:, column(s)], w_v.at[s], ld_w.at[s])

    load_gate = pltpu.make_async_copy(gate_hbm, gate_v, ld_a.at[0])
    load_up = pltpu.make_async_copy(up_hbm, up_v, ld_a.at[1])

    def each(n, f):
        def step(s, carry):
            f(s)
            return carry

        lax.fori_loop(0, n, step, 0)

    each(STEPS, lambda s: load_g(s).start())
    load_gate.start()
    load_up.start()
    each(STEPS, lambda s: load_w(s).start())

    barrier = pltpu.get_barrier_semaphore()
    for device in (to_yp, to_ym, to_z, to_zc, to_core, to_zh, to_x(1), to_x(2), to_x(3)):
        pl.semaphore_signal(barrier, inc=1, device_id=device, device_id_type=MESH)
    pl.semaphore_wait(barrier, 9)

    def remote(src, dst, send, recv, device):
        return pltpu.make_async_remote_copy(
            src_ref=src, dst_ref=dst, send_sem=send, recv_sem=recv,
            device_id=device, device_id_type=MESH,
        )

    ROW_ALL, ROW_A, ROW_B, ROW_C = pl.ds(0, ROWS), pl.ds(0, RA), pl.ds(RA, RB), pl.ds(RAB, RC)
    ROW_AB, ROW_BC = pl.ds(0, RAB), pl.ds(RA, RB + RC)
    COL_ALL, COL_0, COL_1 = pl.ds(0, WIDTH), pl.ds(0, HALF), pl.ds(HALF, HALF)

    gather = (
        (own + y, other + y, ROW_AB, COL_ALL, to_z),
        (own + y, own + ym, ROW_ALL, COL_ALL, to_yp),
        (own + y, own + yp, ROW_ALL, COL_ALL, to_ym),
        (other + y, other + ym, ROW_A, COL_ALL, to_yp),
        (other + y, other + yp, ROW_A, COL_ALL, to_ym),
        (own + yp, own + y2, ROW_ALL, COL_0, to_ym),
        (own + ym, own + y2, ROW_ALL, COL_1, to_yp),
        (own + yp, other + yp, ROW_B, COL_ALL, to_z),
        (own + ym, other + ym, ROW_B, COL_ALL, to_z),
        (other + yp, other + y2, ROW_A, COL_0, to_ym),
        (other + ym, other + y2, ROW_A, COL_1, to_yp),
        (own + y2, other + y2, ROW_B, COL_0, to_z),
        (own + y2, other + y2, ROW_B, COL_1, to_z),
        (own + y, other + y, ROW_C, COL_ALL, to_zc),
        (own + yp, other + yp, ROW_C, COL_ALL, to_zc),
        (own + ym, other + ym, ROW_C, COL_ALL, to_zc),
        (own + y2, other + y2, ROW_C, COL_0, to_zc),
        (own + y2, other + y2, ROW_C, COL_1, to_zc),
    )

    def ag(k, s, arriving=False):
        leaves, arrives, rows, cols, device = gather[k]
        ref = gb.at[s, arrives if arriving else leaves, rows, cols]
        return remote(ref, ref, ag_s.at[k, s], ag_r.at[k, s], device)

    def ag_send(k, s):
        ag(k, s).start()

    def ag_wait(k, s):
        ag(k, s, True).wait_recv()

    HEAD_B, TAIL_C, ALL = pl.ds(0, RB), pl.ds(RB, RC), slice(None)
    reduction = (
        (other + yp, ROW_B, COL_ALL, rz1, 0, HEAD_B, to_z),
        (other + ym, ROW_B, COL_ALL, rz1, 1, HEAD_B, to_z),
        (other + y2, ROW_B, COL_ALL, rz1, 2, HEAD_B, to_z),
        (other + y2, ROW_A, COL_0, rho, 0, ALL, to_yp),
        (other + y2, ROW_A, COL_1, rho, 1, ALL, to_ym),
        (own + y2, ROW_ALL, COL_0, rhw, 0, ALL, to_yp),
        (own + y2, ROW_ALL, COL_1, rhw, 1, ALL, to_ym),
        (other + yp, ROW_A, COL_ALL, rfo, 0, ALL, to_yp),
        (other + ym, ROW_A, COL_ALL, rfo, 1, ALL, to_ym),
        (own + yp, ROW_ALL, COL_ALL, rfw, 0, ALL, to_yp),
        (own + ym, ROW_ALL, COL_ALL, rfw, 1, ALL, to_ym),
        (other + y, ROW_AB, COL_ALL, rz2, 0, ROW_AB, to_z),
        (other + yp, ROW_C, COL_ALL, rz1, 0, TAIL_C, to_zc),
        (other + ym, ROW_C, COL_ALL, rz1, 1, TAIL_C, to_zc),
        (other + y2, ROW_C, COL_ALL, rz1, 2, TAIL_C, to_zc),
        (other + y, ROW_C, COL_ALL, rz2, 0, ROW_C, to_zc),
    )

    def rs(k, s):
        slot, rows, cols, land, index, part, device = reduction[k]
        return remote(
            p.at[s, slot, rows, cols], land.at[s, index, part, :], rs_s.at[k, s], rs_r.at[k, s], device
        )

    def rs_send(k, s):
        rs(k, s).start()

    def rs_wait(k, s):
        rs(k, s).wait_recv()

    def core_copy(s):
        return remote(cs.at[s], cr.at[s], c_s.at[s], c_r.at[s], to_core)

    def x_copy(s):
        return remote(ck.at[s], xr.at[s], x_s.at[s], x_r.at[s], to_x(1 + s // 2))

    zh_copy = remote(zs, zr, zh_s, zh_r, to_zh)
    swapped = h_v.at[pl.ds(other, 4), ROW_C, :]
    h_swap = remote(swapped, hx, sw_s.at[0], sw_r.at[0], to_zh)
    grad_swap = remote(gs, gr, sw_s.at[1], sw_r.at[1], to_zh)

    def a0(s):
        load_g(s).wait()
        for k in (1, 2, 0, 13):
            ag_send(k, s)

    def a1(s):
        ag_wait(0, s)
        ag_send(3, s)
        ag_send(4, s)
        ag_wait(2, s)
        ag_send(5, s)
        ag_send(7, s)
        ag_send(14, s)
        ag_wait(1, s)
        ag_send(6, s)
        ag_send(8, s)
        ag_send(15, s)

    def a2(s):
        ag_wait(4, s)
        ag_send(9, s)
        ag_wait(3, s)
        ag_send(10, s)
        ag_wait(5, s)
        ag_send(11, s)
        ag_send(16, s)
        ag_wait(6, s)
        ag_send(12, s)
        ag_send(17, s)

    def a3(s):
        for k in range(7, 18):
            ag_wait(k, s)

        def weight_half(side, dst):
            cols = pl.ds(pl.multiple_of(side * HALF, HALF), HALF)

            def tile(t, carry):
                rows = pl.ds(pl.multiple_of(t * 448, 64), 448)
                block = gb[s, :, :, cols].reshape(8 * ROWS, HALF)
                product = jnp.dot(ht_v[rows, :], block, preferred_element_type=F32)
                dst[s, rows, :] = (product * scale).astype(BF16)
                return carry

            lax.fori_loop(0, 2, tile, 0)

        weight_half(1 - core, cs)
        core_copy(s).start()
        weight_half(core, ck)

        def tile(t, carry):
            rows = pl.ds(t * 4, 4)
            block = gb[s, rows].reshape(512, WIDTH)
            product = lax.dot_general(
                block, w_v[s], (((1,), (1,)), ((), ())), preferred_element_type=F32
            ).reshape(4, ROWS, FF)

            @pl.when(s == 0)
            def _():
                hg[rows] = product

            @pl.when(s > 0)
            def _():
                hg[rows] += product

            return carry

        lax.fori_loop(0, 2, tile, 0)

    def d1(s):
        core_copy(s).wait_recv()
        add_rows(ck.at[s], [cr.at[s]], FF)

        @pl.when(s < 6)
        def _():
            x_copy(s).start()

    def d2a():
        for k in range(6):
            x_copy(k).wait_recv()

        def tile(t, carry):
            sl = pl.ds(pl.multiple_of(t * 16, 16), 16)
            total = ck[7 - zh, sl, :].astype(F32)
            for k in (0, 2, 4):
                total += xr[k + 1 - zh, sl, :].astype(F32)
            zs[sl, :] = total.astype(BF16)
            return carry

        lax.fori_loop(0, FF // 16, tile, 0)
        zh_copy.start()

    save_d = pltpu.make_async_copy(gd_v, gd_out, st_d)

    def d2b():
        zh_copy.wait_recv()

        def tile(t, carry):
            sl = pl.ds(pl.multiple_of(t * 16, 16), 16)
            total = ck[6 + zh, sl, :].astype(F32) + zr[sl, :].astype(F32)
            for k in (0, 2, 4):
                total += xr[k + zh, sl, :].astype(F32)
            gd_v[sl, :] = total
            return carry

        lax.fori_loop(0, FF // 16, tile, 0)
        save_d.start()

    def r0(s):
        load_w(s).wait()

        def tile(t, carry):
            rows = pl.ds(t * 4, 4)
            product = jnp.dot(
                h_v[rows].reshape(512, FF), w_v[s], preferred_element_type=F32
            )
            p[s, rows] = product.astype(BF16).reshape(4, ROWS, WIDTH)
            return carry

        lax.fori_loop(0, 2, tile, 0)
        for k in (0, 12, 1, 13, 2, 14, 3, 4):
            rs_send(k, s)

    def r1(s):
        for k, slot in ((2, own + y2), (0, own + yp), (1, own + ym)):
            rs_wait(k, s)
            rs_wait(k + 12, s)
            add_rows(p.at[s, slot, ROW_BC, :], [rz1.at[s, k]], RB + RC)
            if k == 2:
                rs_send(5, s)
                rs_send(6, s)

    def r2(s):
        rs_wait(3, s)
        add_rows(p.at[s, other + yp, ROW_A, COL_0], [rho.at[s, 0]], RA)
        rs_send(7, s)
        rs_wait(4, s)
        add_rows(p.at[s, other + ym, ROW_A, COL_1], [rho.at[s, 1]], RA)
        rs_send(8, s)
        rs_wait(5, s)
        add_rows(p.at[s, own + yp, ROW_ALL, COL_0], [rhw.at[s, 0]], ROWS)
        rs_send(9, s)
        rs_wait(6, s)
        add_rows(p.at[s, own + ym, ROW_ALL, COL_1], [rhw.at[s, 1]], ROWS)
        rs_send(10, s)

    def r3(s):
        rs_wait(7, s)
        rs_wait(8, s)
        rs_send(15, s)
        add_rows(p.at[s, other + y, ROW_A, :], [rfo.at[s, 0], rfo.at[s, 1]], RA)
        rs_send(11, s)

    def save_f(s):
        return pltpu.make_async_copy(p.at[s, te], f_out.at[:, column(s)], st_f.at[s])

    def r4(s):
        for k in (9, 10, 11, 15):
            rs_wait(k, s)
        add_rows(p.at[s, te], [rfw.at[s, 0], rfw.at[s, 1], rz2.at[s, 0]], ROWS)
        save_f(s).start()

    def save_e(e, which):
        first = jnp.where(e < 2, own, other) + (e % 2) * 2
        rows = pl.ds(pl.multiple_of(first * ROWS, 2 * ROWS), 2 * ROWS)
        src, dst = ((gate_v, gg_out), (up_v, gu_out))[which]
        return pltpu.make_async_copy(src.at[rows, :], dst.at[rows, :], st_e.at[which, e])

    def e0(e):
        first = jnp.where(e < 2, own, other) + (e % 2) * 2

        def tile(t, carry):
            slot = first + t // 8
            row = pl.multiple_of((t % 8) * 16, 16)
            sl = pl.ds(pl.multiple_of(slot * ROWS + row, 16), 16)
            g = gate_v[sl, :].astype(F32)
            u = up_v[sl, :].astype(F32)
            grad = hg[slot, pl.ds(row, 16), :]
            s = jax.nn.sigmoid(g)
            gate_v[sl, :] = (grad * u * s * (1.0 + g * (1.0 - s))).astype(BF16)
            up_v[sl, :] = (grad * (g * s)).astype(BF16)
            return carry

        lax.fori_loop(0, 16, tile, 0)
        save_e(e, 0).start()
        save_e(e, 1).start()

    def swap_tiles(f):
        def tile(t, carry):
            row = pl.multiple_of((t % 3) * 16, 16)
            f(t // 3, pl.ds(row, 16), pl.ds(RAB + row, 16))
            return carry

        lax.fori_loop(0, 4 * (RC // 16), tile, 0)

    def gx():
        def move(k, part, row):
            gs[k, part, :] = hg[other + k, row, :].astype(BF16)

        swap_tiles(move)
        grad_swap.start()

    def gr_stage():
        grad_swap.wait_recv()

        def move(k, part, row):
            hg[other + k, row, :] = gr[k, part, :].astype(F32)

        swap_tiles(move)

    def hidden_rows(slot, row, count):
        def tile(t, carry):
            start = pl.multiple_of(row + t * 16, 16)
            sl = pl.ds(pl.multiple_of(slot * ROWS + start, 16), 16)
            g = gate_v[sl, :].astype(F32)
            u = up_v[sl, :].astype(F32)
            h_v[slot, pl.ds(start, 16), :] = (g * jax.nn.sigmoid(g) * u).astype(BF16)
            return carry

        lax.fori_loop(0, count // 16, tile, 0)

    def hx_stage():
        h_swap.wait_send()
        h_swap.wait_recv()

        def move(k, part, row):
            h_v[other + k, row, :] = hx[k, part, :]

        swap_tiles(move)

        def transpose_tile(t, carry):
            ht_v[:, pl.ds(pl.multiple_of(t * ROWS, ROWS), ROWS)] = h_v[t].T
            return carry

        lax.fori_loop(0, 8, transpose_tile, 0)

    each(LOOKAHEAD, a0)
    load_gate.wait()
    load_up.wait()

    each(4, lambda k: hidden_rows(other + k, RAB, RC))
    h_swap.start()
    each(4, lambda k: hidden_rows(own + k, 0, ROWS))
    each(4, lambda k: hidden_rows(other + k, 0, RAB))

    def iteration(i, carry):
        def stage(name, f, count=STEPS):
            s = i - OFF[name]

            @pl.when((s >= 0) & (s < count))
            def _():
                f(s)

        @pl.when(i + LOOKAHEAD < STEPS)
        def _():
            a0(i + LOOKAHEAD)

        stage("A1", a1)
        stage("A2", a2)
        stage("HX", lambda s: hx_stage(), 1)
        stage("R0", r0)
        stage("R1", r1)
        stage("R2", r2)
        stage("R3", r3)
        stage("A3", a3)
        stage("GX", lambda s: gx(), 1)
        stage("D1", d1)
        stage("D2A", lambda s: d2a(), 1)
        stage("R4", r4)
        stage("GR", lambda s: gr_stage(), 1)
        stage("E", e0, 4)
        stage("D2B", lambda s: d2b(), 1)
        return carry

    lax.fori_loop(0, ITERS, iteration, 0)

    def finish(s):
        for k in range(18):
            ag(k, s).wait_send()
        for k in range(16):
            rs(k, s).wait_send()
        core_copy(s).wait_send()
        save_f(s).wait()

    each(STEPS, finish)
    each(6, lambda s: x_copy(s).wait_send())
    zh_copy.wait_send()
    grad_swap.wait_send()

    def finish_e(e):
        save_e(e, 0).wait()
        save_e(e, 1).wait()

    each(4, finish_e)
    save_d.wait()


PIECES = 4


def settle_kernel(a0, a1, a2, a3, b0, b1, b2, b3, v0, v1, v2, v3, load_sem, save_sem):
    pieces = []
    for k, (src, mid, dst) in enumerate(((a1, v1, b1), (a2, v2, b2), (a0, v0, b0), (a3, v3, b3))):
        count = src.shape[0] // PIECES
        for part in range(PIECES):
            rows = pl.ds(part * count, count)
            n = k * PIECES + part
            pieces.append((
                pltpu.make_async_copy(src.at[rows, :], mid.at[rows, :], load_sem.at[n]),
                pltpu.make_async_copy(mid.at[rows, :], dst.at[rows, :], save_sem.at[n]),
            ))
    for load, _ in pieces:
        load.start()
    for load, save in pieces:
        load.wait()
        save.start()
    for _, save in pieces:
        save.wait()


def settle(outs):
    anywhere = pl.BlockSpec(memory_space=pl.ANY)
    return pl.pallas_call(
        settle_kernel,
        out_shape=tuple(jax.ShapeDtypeStruct(o.shape, o.dtype) for o in outs),
        in_specs=[anywhere] * 4,
        out_specs=[anywhere] * 4,
        scratch_shapes=[pltpu.VMEM(o.shape, o.dtype) for o in outs]
        + [pltpu.SemaphoreType.DMA((4 * PIECES,))] * 2,
        compiler_params=pltpu.CompilerParams(vmem_limit_bytes=60 * 1024 * 1024),
        cost_estimate=pl.CostEstimate(flops=0, bytes_accessed=11_000_000, transcendentals=0),
    )(*outs)


def body(gate_pre, up_pre, down_weight, grad_out):
    replica_rows, ff = gate_pre.shape
    rows, width = grad_out.shape
    scale = 1.0 / math.sqrt(replica_rows * lax.axis_size("dp"))
    vmem, dma = pltpu.VMEM, pltpu.SemaphoreType.DMA
    anywhere = pl.BlockSpec(memory_space=pl.ANY)
    outs = pl.pallas_call(
        functools.partial(kernel, scale),
        out_shape=(
            jax.ShapeDtypeStruct((rows, width), BF16),
            jax.ShapeDtypeStruct((replica_rows, ff), BF16),
            jax.ShapeDtypeStruct((replica_rows, ff), BF16),
            jax.ShapeDtypeStruct((ff, width // 16), F32),
        ),
        in_specs=[anywhere] * 4,
        out_specs=[anywhere] * 4,
        scratch_shapes=[
            vmem((replica_rows, ff), BF16),
            vmem((replica_rows, ff), BF16),
            vmem((STEPS, ff, WIDTH), BF16),
            vmem((8, ROWS, ff), BF16),
            vmem((ff, replica_rows), BF16),
            vmem((STEPS, 8, ROWS, WIDTH), BF16),
            vmem((STEPS, 8, ROWS, WIDTH), BF16),
            vmem((8, ROWS, ff), F32),
            vmem((STEPS, 3, RB + RC, WIDTH), BF16),
            vmem((STEPS, 2, RA, HALF), BF16),
            vmem((STEPS, 2, ROWS, HALF), BF16),
            vmem((STEPS, 2, RA, WIDTH), BF16),
            vmem((STEPS, 2, ROWS, WIDTH), BF16),
            vmem((STEPS, 1, ROWS, WIDTH), BF16),
            vmem((4, RC, ff), BF16),
            vmem((4, RC, ff), BF16),
            vmem((4, RC, ff), BF16),
            vmem((STEPS, ff, HALF), BF16),
            vmem((STEPS, ff, HALF), BF16),
            vmem((STEPS, ff, HALF), BF16),
            vmem((6, ff, HALF), BF16),
            vmem((ff, HALF), BF16),
            vmem((ff, HALF), BF16),
            vmem((ff, HALF), F32),
            dma((18, STEPS)), dma((18, STEPS)),
            dma((16, STEPS)), dma((16, STEPS)),
            dma((STEPS,)), dma((STEPS,)),
            dma((6,)), dma((6,)),
            dma, dma,
            dma((2,)), dma((2,)),
            dma((STEPS,)), dma((STEPS,)), dma((2,)),
            dma((STEPS,)), dma((2, 4)), dma,
        ],
        compiler_params=pltpu.CompilerParams(
            collective_id=0, has_side_effects=True, vmem_limit_bytes=60 * 1024 * 1024
        ),
        cost_estimate=pl.CostEstimate(
            flops=6 * replica_rows * ff * width, bytes_accessed=20_000_000, transcendentals=2_000_000
        ),
    )(gate_pre, up_pre, down_weight, grad_out)
    return settle(outs)


def solution(mesh):
    return jax.shard_map(
        body,
        mesh=mesh,
        in_specs=(
            P("dp", "tensor"),
            P("dp", "tensor"),
            P("tensor", None),
            P(("dp", "tensor"), None),
        ),
        out_specs=(
            P(("dp", "tensor"), None),
            P("dp", "tensor"),
            P("dp", "tensor"),
            P("tensor", "dp"),
        ),
        check_vma=False,
    )
```

```python
import functools
import math

import jax
import jax.numpy as jnp
from jax import lax
from jax.experimental import pallas as pl
from jax.experimental.pallas import tpu as pltpu
from jax.sharding import PartitionSpec as P

MESH = pl.DeviceIdType.MESH
F32 = jnp.float32
BF16 = jnp.bfloat16

GATHER_GROUP = (0, 1, 1, 2, 2, 3, 3) + (4,) * 11
REDUCE_GROUP = (0, 0, 0, 1, 1, 2, 2, 3, 3, 4, 4, 4, 0, 0, 0, 4)

STEPS = 8
WIDTH = 512
HALF = 256
ROWS = 128
RA = 48
RB = 32
RC = 48
RAB = RA + RB
FF = 896

LOOKAHEAD = 3
OFF = dict(A1=0, HX=1, A2=1, A3=2, D1=3, R0=1, R1=2, R2=4, R3=5, R4=6, GX=9, GR=11, E=10, D2A=10, D2B=12)
ITERS = 14


def add_rows(dst, srcs, rows):
    def step(t, carry):
        sl = pl.ds(pl.multiple_of(t * 16, 16), 16)
        total = dst[sl, :].astype(F32)
        for src in srcs:
            total += src[sl, :].astype(F32)
        dst[sl, :] = total.astype(dst.dtype)
        return carry

    lax.fori_loop(0, rows // 16, step, 0)


def kernel(
    scale,
    gate_hbm, up_hbm, w_hbm, g_hbm,
    f_out, gg_out, gu_out, gd_out,
    gate_v, up_v, w_v, h_v, ht_v, gb, p, hg,
    rz1, rho, rhw, rfo, rfw, rz2,
    hx, gs, gr,
    cs, ck, cr, xr, zs, zr, gd_v,
    ag_s, ag_r, rs_s, rs_r, c_s, c_r, x_s, x_r, zh_s, zh_r, sw_s, sw_r,
    ld_g, ld_w, ld_a, st_f, st_e, st_d,
):
    dp = lax.axis_index("dp")
    te = lax.axis_index("tensor")
    x, zh, core = dp // 4, (dp // 2) % 2, dp % 2
    z, y = te // 4, te % 4
    yp, ym, y2 = (y + 1) % 4, (y + 3) % 4, (y + 2) % 4
    zo = 1 - z
    own, other = z * 4, zo * 4
    to_yp, to_ym, to_z = (dp, own + yp), (dp, own + ym), (dp, other + y)
    to_core = (x * 4 + zh * 2 + (1 - core), te)
    to_zh = (x * 4 + (1 - zh) * 2 + core, te)
    to_zc = (x * 4 + (1 - zh) * 2 + core, other + y)

    def to_x(d):
        return (((x + d) % 4) * 4 + zh * 2 + core, te)

    def distance(s):
        return jnp.where(s < 4, 1 + 2 * (s % 2), jnp.where(s < 6, 2, 0))

    def column(s):
        j = 2 * ((x + distance(s)) % 4) + jnp.where(s < 4, s // 2, s % 2)
        return pl.ds(pl.multiple_of(j * WIDTH, WIDTH), WIDTH)

    def load_g(s):
        return pltpu.make_async_copy(g_hbm.at[:, column(s)], gb.at[s, te], ld_g)

    def load_w(s):
        return pltpu.make_async_copy(w_hbm.at[:, column(s)], w_v.at[s], ld_w)

    load_gate = pltpu.make_async_copy(gate_hbm, gate_v, ld_a.at[0])
    load_up = pltpu.make_async_copy(up_hbm, up_v, ld_a.at[1])

    def each(n, f):
        def step(s, carry):
            f(s)
            return carry

        lax.fori_loop(0, n, step, 0)

    each(STEPS, lambda s: load_g(s).start())
    load_gate.start()
    load_up.start()
    each(STEPS, lambda s: load_w(s).start())

    barrier = pltpu.get_barrier_semaphore()
    for device in (to_yp, to_ym, to_z, to_zc, to_core, to_zh, to_x(1), to_x(2), to_x(3)):
        pl.semaphore_signal(barrier, inc=1, device_id=device, device_id_type=MESH)
    pl.semaphore_wait(barrier, 9)

    def remote(src, dst, send, recv, device):
        return pltpu.make_async_remote_copy(
            src_ref=src, dst_ref=dst, send_sem=send, recv_sem=recv,
            device_id=device, device_id_type=MESH,
        )

    ROW_ALL, ROW_A, ROW_B, ROW_C = pl.ds(0, ROWS), pl.ds(0, RA), pl.ds(RA, RB), pl.ds(RAB, RC)
    ROW_AB, ROW_BC = pl.ds(0, RAB), pl.ds(RA, RB + RC)
    COL_ALL, COL_0, COL_1 = pl.ds(0, WIDTH), pl.ds(0, HALF), pl.ds(HALF, HALF)

    gather = (
        (own + y, other + y, ROW_AB, COL_ALL, to_z),
        (own + y, own + ym, ROW_ALL, COL_ALL, to_yp),
        (own + y, own + yp, ROW_ALL, COL_ALL, to_ym),
        (other + y, other + ym, ROW_A, COL_ALL, to_yp),
        (other + y, other + yp, ROW_A, COL_ALL, to_ym),
        (own + yp, own + y2, ROW_ALL, COL_0, to_ym),
        (own + ym, own + y2, ROW_ALL, COL_1, to_yp),
        (own + yp, other + yp, ROW_B, COL_ALL, to_z),
        (own + ym, other + ym, ROW_B, COL_ALL, to_z),
        (other + yp, other + y2, ROW_A, COL_0, to_ym),
        (other + ym, other + y2, ROW_A, COL_1, to_yp),
        (own + y2, other + y2, ROW_B, COL_0, to_z),
        (own + y2, other + y2, ROW_B, COL_1, to_z),
        (own + y, other + y, ROW_C, COL_ALL, to_zc),
        (own + yp, other + yp, ROW_C, COL_ALL, to_zc),
        (own + ym, other + ym, ROW_C, COL_ALL, to_zc),
        (own + y2, other + y2, ROW_C, COL_0, to_zc),
        (own + y2, other + y2, ROW_C, COL_1, to_zc),
    )

    def ag_send(k, s):
        leaves, _, rows, cols, device = gather[k]
        ref = gb.at[s, leaves, rows, cols]
        remote(ref, ref, ag_s.at[s], ag_r.at[GATHER_GROUP[k], s], device).start()

    def arrived(ref, sem):
        remote(ref, ref, sem, sem, to_z).wait_recv()

    def left(ref, sem):
        remote(ref, ref, sem, sem, to_z).wait_send()

    def ag_wait(group, s):
        ref = (
            gb.at[s, 0, ROW_AB, :],
            gb.at[s, pl.ds(0, 2)],
            gb.at[s, pl.ds(0, 2), ROW_A, :],
            gb.at[s, 0],
            gb.at[s, pl.ds(0, 3), pl.ds(0, 112), :],
        )[group]
        arrived(ref, ag_r.at[group, s])

    HEAD_B, TAIL_C, ALL = pl.ds(0, RB), pl.ds(RB, RC), slice(None)
    reduction = (
        (other + yp, ROW_B, COL_ALL, rz1, 0, HEAD_B, to_z),
        (other + ym, ROW_B, COL_ALL, rz1, 1, HEAD_B, to_z),
        (other + y2, ROW_B, COL_ALL, rz1, 2, HEAD_B, to_z),
        (other + y2, ROW_A, COL_0, rho, 0, ALL, to_yp),
        (other + y2, ROW_A, COL_1, rho, 1, ALL, to_ym),
        (own + y2, ROW_ALL, COL_0, rhw, 0, ALL, to_yp),
        (own + y2, ROW_ALL, COL_1, rhw, 1, ALL, to_ym),
        (other + yp, ROW_A, COL_ALL, rfo, 0, ALL, to_yp),
        (other + ym, ROW_A, COL_ALL, rfo, 1, ALL, to_ym),
        (own + yp, ROW_ALL, COL_ALL, rfw, 0, ALL, to_yp),
        (own + ym, ROW_ALL, COL_ALL, rfw, 1, ALL, to_ym),
        (other + y, ROW_AB, COL_ALL, rz2, 0, ROW_AB, to_z),
        (other + yp, ROW_C, COL_ALL, rz1, 0, TAIL_C, to_zc),
        (other + ym, ROW_C, COL_ALL, rz1, 1, TAIL_C, to_zc),
        (other + y2, ROW_C, COL_ALL, rz1, 2, TAIL_C, to_zc),
        (other + y, ROW_C, COL_ALL, rz2, 0, ROW_C, to_zc),
    )

    def rs_send(k, s):
        slot, rows, cols, land, index, part, device = reduction[k]
        remote(
            p.at[s, slot, rows, cols], land.at[s, index, part, :],
            rs_s.at[s], rs_r.at[REDUCE_GROUP[k], s], device,
        ).start()

    def rs_wait(group, s):
        ref = (
            p.at[s, pl.ds(0, 3), ROW_AB, :],
            p.at[s, 0, ROW_A, :],
            p.at[s, 0],
            p.at[s, pl.ds(0, 2), ROW_A, :],
            p.at[s, pl.ds(0, 3)],
        )[group]
        arrived(ref, rs_r.at[group, s])

    def core_copy(s):
        return remote(cs.at[s], cr.at[s], c_s, c_r.at[s], to_core)

    def x_copy(s):
        return remote(ck.at[s], xr.at[s], x_s, x_r, to_x(distance(s)))

    zh_copy = remote(zs, zr, zh_s, zh_r, to_zh)
    swapped = h_v.at[pl.ds(other, 4), ROW_C, :]
    h_swap = remote(swapped, hx, sw_s.at[0], sw_r.at[0], to_zh)
    grad_swap = remote(gs, gr, sw_s.at[1], sw_r.at[1], to_zh)

    def a0(s):
        for k in (1, 2, 0, 13):
            ag_send(k, s)

    def a1(s):
        ag_wait(0, s)
        ag_send(3, s)
        ag_send(4, s)
        ag_wait(1, s)
        for k in (5, 6, 7, 8, 14, 15):
            ag_send(k, s)

    def a2(s):
        ag_wait(2, s)
        ag_send(9, s)
        ag_send(10, s)
        ag_wait(3, s)
        for k in (11, 12, 16, 17):
            ag_send(k, s)

    def a3(s):
        ag_wait(4, s)

        def weight_half(side, dst):
            cols = pl.ds(pl.multiple_of(side * HALF, HALF), HALF)

            def tile(t, carry):
                rows = pl.ds(pl.multiple_of(t * 448, 64), 448)
                block = gb[s, :, :, cols].reshape(8 * ROWS, HALF)
                product = jnp.dot(ht_v[rows, :], block, preferred_element_type=F32)
                dst[s, rows, :] = (product * scale).astype(BF16)
                return carry

            lax.fori_loop(0, 2, tile, 0)

        weight_half(1 - core, cs)
        core_copy(s).start()
        weight_half(core, ck)

        def tile(t, carry):
            rows = pl.ds(t * 4, 4)
            block = gb[s, rows].reshape(512, WIDTH)
            product = lax.dot_general(
                block, w_v[s], (((1,), (1,)), ((), ())), preferred_element_type=F32
            ).reshape(4, ROWS, FF)

            @pl.when(s == 0)
            def _():
                hg[rows] = product

            @pl.when(s > 0)
            def _():
                hg[rows] += product

            return carry

        lax.fori_loop(0, 2, tile, 0)

    def d1(s):
        core_copy(s).wait_recv()
        add_rows(ck.at[s], [cr.at[s]], FF)

        @pl.when(s < 6)
        def _():
            x_copy(s).start()

    def d2a():
        arrived(xr, x_r)

        def tile(t, carry):
            sl = pl.ds(pl.multiple_of(t * 16, 16), 16)
            total = ck[7 - zh, sl, :].astype(F32)
            for k, d in ((0, 2), (1, 2), (4, 1)):
                total += xr[k + (1 - zh) * d, sl, :].astype(F32)
            zs[sl, :] = total.astype(BF16)
            return carry

        lax.fori_loop(0, FF // 16, tile, 0)
        zh_copy.start()

    save_d = pltpu.make_async_copy(gd_v, gd_out, st_d)

    def d2b():
        zh_copy.wait_recv()

        def tile(t, carry):
            sl = pl.ds(pl.multiple_of(t * 16, 16), 16)
            total = ck[6 + zh, sl, :].astype(F32) + zr[sl, :].astype(F32)
            for k, d in ((0, 2), (1, 2), (4, 1)):
                total += xr[k + zh * d, sl, :].astype(F32)
            gd_v[sl, :] = total
            return carry

        lax.fori_loop(0, FF // 16, tile, 0)
        save_d.start()

    def r0(s):
        def tile(t, carry):
            rows = pl.ds(t * 4, 4)
            product = jnp.dot(
                h_v[rows].reshape(512, FF), w_v[s], preferred_element_type=F32
            )
            p[s, rows] = product.astype(BF16).reshape(4, ROWS, WIDTH)
            return carry

        lax.fori_loop(0, 2, tile, 0)
        for k in (0, 12, 1, 13, 2, 14, 3, 4):
            rs_send(k, s)

    def r1(s):
        rs_wait(0, s)
        for k, slot in ((2, own + y2), (0, own + yp), (1, own + ym)):
            add_rows(p.at[s, slot, ROW_BC, :], [rz1.at[s, k]], RB + RC)
            if k == 2:
                rs_send(5, s)
                rs_send(6, s)

    def r2(s):
        rs_wait(1, s)
        add_rows(p.at[s, other + yp, ROW_A, COL_0], [rho.at[s, 0]], RA)
        rs_send(7, s)
        add_rows(p.at[s, other + ym, ROW_A, COL_1], [rho.at[s, 1]], RA)
        rs_send(8, s)
        rs_wait(2, s)
        add_rows(p.at[s, own + yp, ROW_ALL, COL_0], [rhw.at[s, 0]], ROWS)
        rs_send(9, s)
        add_rows(p.at[s, own + ym, ROW_ALL, COL_1], [rhw.at[s, 1]], ROWS)
        rs_send(10, s)

    def r3(s):
        rs_send(15, s)
        rs_wait(3, s)
        add_rows(p.at[s, other + y, ROW_A, :], [rfo.at[s, 0], rfo.at[s, 1]], RA)
        rs_send(11, s)

    def save_f(s):
        return pltpu.make_async_copy(p.at[s, te], f_out.at[:, column(s)], st_f)

    def r4(s):
        rs_wait(4, s)
        add_rows(p.at[s, te], [rfw.at[s, 0], rfw.at[s, 1], rz2.at[s, 0]], ROWS)
        save_f(s).start()

    def save_e(e, which):
        first = jnp.where(e < 2, own, other) + (e % 2) * 2
        rows = pl.ds(pl.multiple_of(first * ROWS, 2 * ROWS), 2 * ROWS)
        src, dst = ((gate_v, gg_out), (up_v, gu_out))[which]
        return pltpu.make_async_copy(src.at[rows, :], dst.at[rows, :], st_e.at[which])

    def e0(e):
        first = jnp.where(e < 2, own, other) + (e % 2) * 2

        def tile(t, carry):
            slot = first + t // 8
            row = pl.multiple_of((t % 8) * 16, 16)
            sl = pl.ds(pl.multiple_of(slot * ROWS + row, 16), 16)
            g = gate_v[sl, :].astype(F32)
            u = up_v[sl, :].astype(F32)
            grad = hg[slot, pl.ds(row, 16), :]
            s = jax.nn.sigmoid(g)
            gate_v[sl, :] = (grad * u * s * (1.0 + g * (1.0 - s))).astype(BF16)
            up_v[sl, :] = (grad * (g * s)).astype(BF16)
            return carry

        lax.fori_loop(0, 16, tile, 0)
        save_e(e, 0).start()
        save_e(e, 1).start()

    def swap_tiles(f):
        def tile(t, carry):
            row = pl.multiple_of((t % 3) * 16, 16)
            f(t // 3, pl.ds(row, 16), pl.ds(RAB + row, 16))
            return carry

        lax.fori_loop(0, 4 * (RC // 16), tile, 0)

    def gx():
        def move(k, part, row):
            gs[k, part, :] = hg[other + k, row, :].astype(BF16)

        swap_tiles(move)
        grad_swap.start()

    def gr_stage():
        grad_swap.wait_recv()

        def move(k, part, row):
            hg[other + k, row, :] = gr[k, part, :].astype(F32)

        swap_tiles(move)

    def hidden_rows(slot, row, count):
        def tile(t, carry):
            start = pl.multiple_of(row + t * 16, 16)
            sl = pl.ds(pl.multiple_of(slot * ROWS + start, 16), 16)
            g = gate_v[sl, :].astype(F32)
            u = up_v[sl, :].astype(F32)
            h_v[slot, pl.ds(start, 16), :] = (g * jax.nn.sigmoid(g) * u).astype(BF16)
            return carry

        lax.fori_loop(0, count // 16, tile, 0)

    def hx_stage():
        pltpu.make_async_copy(w_v, w_v, ld_w).wait()
        h_swap.wait_send()
        h_swap.wait_recv()

        def move(k, part, row):
            h_v[other + k, row, :] = hx[k, part, :]

        swap_tiles(move)

        def transpose_tile(t, carry):
            ht_v[:, pl.ds(pl.multiple_of(t * ROWS, ROWS), ROWS)] = h_v[t].T
            return carry

        lax.fori_loop(0, 8, transpose_tile, 0)

    pltpu.make_async_copy(gb.at[:, te], gb.at[:, te], ld_g).wait()
    each(LOOKAHEAD, a0)
    load_gate.wait()
    load_up.wait()

    each(4, lambda k: hidden_rows(other + k, RAB, RC))
    h_swap.start()
    each(4, lambda k: hidden_rows(own + k, 0, ROWS))
    each(4, lambda k: hidden_rows(other + k, 0, RAB))

    def iteration(i, carry):
        def stage(name, f, count=STEPS):
            s = i - OFF[name]

            @pl.when((s >= 0) & (s < count))
            def _():
                f(s)

        @pl.when(i + LOOKAHEAD < STEPS)
        def _():
            a0(i + LOOKAHEAD)

        stage("A1", a1)
        stage("A2", a2)
        stage("HX", lambda s: hx_stage(), 1)
        stage("R0", r0)
        stage("R1", r1)
        stage("R2", r2)
        stage("R3", r3)
        stage("A3", a3)
        stage("GX", lambda s: gx(), 1)
        stage("D1", d1)
        stage("D2A", lambda s: d2a(), 1)
        stage("R4", r4)
        stage("GR", lambda s: gr_stage(), 1)
        stage("E", e0, 4)
        stage("D2B", lambda s: d2b(), 1)
        return carry

    lax.fori_loop(0, ITERS, iteration, 0)

    def finish(s):
        left(gb.at[s, pl.ds(0, 7)], ag_s.at[s])
        left(p.at[s, pl.ds(0, 7)], rs_s.at[s])

    each(STEPS, finish)
    left(cs, c_s)
    left(xr, x_s)
    zh_copy.wait_send()
    grad_swap.wait_send()
    pltpu.make_async_copy(p.at[:, te], p.at[:, te], st_f).wait()
    pltpu.make_async_copy(gate_v, gg_out, st_e.at[0]).wait()
    pltpu.make_async_copy(up_v, gu_out, st_e.at[1]).wait()
    save_d.wait()


PIECES = 4


def settle_kernel(a0, a1, a2, a3, b0, b1, b2, b3, v0, v1, v2, v3, load_sem, save_sem):
    pieces = []
    for k, (src, mid, dst) in enumerate(((a1, v1, b1), (a2, v2, b2), (a0, v0, b0), (a3, v3, b3))):
        count = src.shape[0] // PIECES
        for part in range(PIECES):
            rows = pl.ds(part * count, count)
            n = k * PIECES + part
            pieces.append((
                pltpu.make_async_copy(src.at[rows, :], mid.at[rows, :], load_sem.at[n]),
                pltpu.make_async_copy(mid.at[rows, :], dst.at[rows, :], save_sem.at[n]),
            ))
    for load, _ in pieces:
        load.start()
    for load, save in pieces:
        load.wait()
        save.start()
    for _, save in pieces:
        save.wait()


def settle(outs):
    anywhere = pl.BlockSpec(memory_space=pl.ANY)
    return pl.pallas_call(
        settle_kernel,
        out_shape=tuple(jax.ShapeDtypeStruct(o.shape, o.dtype) for o in outs),
        in_specs=[anywhere] * 4,
        out_specs=[anywhere] * 4,
        scratch_shapes=[pltpu.VMEM(o.shape, o.dtype) for o in outs]
        + [pltpu.SemaphoreType.DMA((4 * PIECES,))] * 2,
        compiler_params=pltpu.CompilerParams(vmem_limit_bytes=60 * 1024 * 1024),
        cost_estimate=pl.CostEstimate(flops=0, bytes_accessed=11_000_000, transcendentals=0),
    )(*outs)


def body(gate_pre, up_pre, down_weight, grad_out):
    replica_rows, ff = gate_pre.shape
    rows, width = grad_out.shape
    scale = 1.0 / math.sqrt(replica_rows * lax.axis_size("dp"))
    vmem, dma = pltpu.VMEM, pltpu.SemaphoreType.DMA
    anywhere = pl.BlockSpec(memory_space=pl.ANY)
    outs = pl.pallas_call(
        functools.partial(kernel, scale),
        out_shape=(
            jax.ShapeDtypeStruct((rows, width), BF16),
            jax.ShapeDtypeStruct((replica_rows, ff), BF16),
            jax.ShapeDtypeStruct((replica_rows, ff), BF16),
            jax.ShapeDtypeStruct((ff, width // 16), F32),
        ),
        in_specs=[anywhere] * 4,
        out_specs=[anywhere] * 4,
        scratch_shapes=[
            vmem((replica_rows, ff), BF16),
            vmem((replica_rows, ff), BF16),
            vmem((STEPS, ff, WIDTH), BF16),
            vmem((8, ROWS, ff), BF16),
            vmem((ff, replica_rows), BF16),
            vmem((STEPS, 8, ROWS, WIDTH), BF16),
            vmem((STEPS, 8, ROWS, WIDTH), BF16),
            vmem((8, ROWS, ff), F32),
            vmem((STEPS, 3, RB + RC, WIDTH), BF16),
            vmem((STEPS, 2, RA, HALF), BF16),
            vmem((STEPS, 2, ROWS, HALF), BF16),
            vmem((STEPS, 2, RA, WIDTH), BF16),
            vmem((STEPS, 2, ROWS, WIDTH), BF16),
            vmem((STEPS, 1, ROWS, WIDTH), BF16),
            vmem((4, RC, ff), BF16),
            vmem((4, RC, ff), BF16),
            vmem((4, RC, ff), BF16),
            vmem((STEPS, ff, HALF), BF16),
            vmem((STEPS, ff, HALF), BF16),
            vmem((STEPS, ff, HALF), BF16),
            vmem((6, ff, HALF), BF16),
            vmem((ff, HALF), BF16),
            vmem((ff, HALF), BF16),
            vmem((ff, HALF), F32),
            dma((STEPS,)), dma((5, STEPS)),
            dma((STEPS,)), dma((5, STEPS)),
            dma, dma((STEPS,)),
            dma, dma,
            dma, dma,
            dma((2,)), dma((2,)),
            dma, dma, dma((2,)),
            dma, dma((2,)), dma,
        ],
        compiler_params=pltpu.CompilerParams(
            collective_id=0, has_side_effects=True, vmem_limit_bytes=60 * 1024 * 1024
        ),
        cost_estimate=pl.CostEstimate(
            flops=6 * replica_rows * ff * width, bytes_accessed=20_000_000, transcendentals=2_000_000
        ),
    )(gate_pre, up_pre, down_weight, grad_out)
    return settle(outs)


def solution(mesh):
    return jax.shard_map(
        body,
        mesh=mesh,
        in_specs=(
            P("dp", "tensor"),
            P("dp", "tensor"),
            P("tensor", None),
            P(("dp", "tensor"), None),
        ),
        out_specs=(
            P(("dp", "tensor"), None),
            P("dp", "tensor"),
            P("dp", "tensor"),
            P("tensor", "dp"),
        ),
        check_vma=False,
    )
```

```python
import functools
import math

import jax
import jax.numpy as jnp
from jax import lax
from jax.experimental import pallas as pl
from jax.experimental.pallas import tpu as pltpu
from jax.sharding import PartitionSpec as P

MESH = pl.DeviceIdType.MESH
F32 = jnp.float32
BF16 = jnp.bfloat16

GATHER_GROUP = (0, 1, 1, 2, 2, 3, 3) + (4,) * 11
REDUCE_GROUP = (0, 0, 0, 1, 1, 2, 2, 3, 3, 4, 4, 4, 0, 0, 0, 4)

STEPS = 8
WIDTH = 512
HALF = 256
ROWS = 128
RA = 48
RB = 32
RC = 48
RAB = RA + RB
FF = 896

LOOKAHEAD = 3
OFF = dict(A1=0, HX=1, A2=1, A3=2, D1=3, R0=2, R1=4, R2=6, R3=8, R4=10, GX=9, GR=11, E=10, D2A=11, D2B=16)
ITERS = 18


def add_rows(dst, srcs, rows):
    def step(t, carry):
        sl = pl.ds(pl.multiple_of(t * 16, 16), 16)
        total = dst[sl, :].astype(F32)
        for src in srcs:
            total += src[sl, :].astype(F32)
        dst[sl, :] = total.astype(dst.dtype)
        return carry

    lax.fori_loop(0, rows // 16, step, 0)


def kernel(
    scale,
    gate_hbm, up_hbm, w_hbm, g_hbm,
    f_out, gg_out, gu_out, gd_out,
    gate_v, up_v, w_v, h_v, ht_v, gb, p, hg,
    rz1, rho, rhw, rfo, rfw, rz2,
    hx, gs, gr,
    cs, ck, cr, xr, zs, zr, gd_v,
    ag_s, ag_r, rs_s, rs_r, c_s, c_r, x_s, x_r, zh_s, zh_r, sw_s, sw_r,
    ld_g, ld_w, ld_a, st_f, st_e, st_d,
):
    dp = lax.axis_index("dp")
    te = lax.axis_index("tensor")
    x, zh, core = dp // 4, (dp // 2) % 2, dp % 2
    z, y = te // 4, te % 4
    yp, ym, y2 = (y + 1) % 4, (y + 3) % 4, (y + 2) % 4
    zo = 1 - z
    own, other = z * 4, zo * 4
    to_yp, to_ym, to_z = (dp, own + yp), (dp, own + ym), (dp, other + y)
    to_core = (x * 4 + zh * 2 + (1 - core), te)
    to_zh = (x * 4 + (1 - zh) * 2 + core, te)
    to_zc = (x * 4 + (1 - zh) * 2 + core, other + y)

    def to_x(d):
        return (((x + d) % 4) * 4 + zh * 2 + core, te)

    def distance(s):
        return jnp.where(s < 4, 1 + 2 * (s % 2), jnp.where(s < 6, 2, 0))

    def column(s):
        j = 2 * ((x + distance(s)) % 4) + jnp.where(s < 4, s // 2, s % 2)
        return pl.ds(pl.multiple_of(j * WIDTH, WIDTH), WIDTH)

    def load_g(s):
        return pltpu.make_async_copy(g_hbm.at[:, column(s)], gb.at[s, te], ld_g)

    def load_w(s):
        return pltpu.make_async_copy(w_hbm.at[:, column(s)], w_v.at[s], ld_w)

    load_gate = pltpu.make_async_copy(gate_hbm, gate_v, ld_a.at[0])
    load_up = pltpu.make_async_copy(up_hbm, up_v, ld_a.at[1])

    def each(n, f):
        def step(s, carry):
            f(s)
            return carry

        lax.fori_loop(0, n, step, 0)

    each(STEPS, lambda s: load_g(s).start())
    load_gate.start()
    load_up.start()
    each(STEPS, lambda s: load_w(s).start())

    barrier = pltpu.get_barrier_semaphore()
    for device in (to_yp, to_ym, to_z, to_zc, to_core, to_zh, to_x(1), to_x(2), to_x(3)):
        pl.semaphore_signal(barrier, inc=1, device_id=device, device_id_type=MESH)
    pl.semaphore_wait(barrier, 9)

    def remote(src, dst, send, recv, device):
        return pltpu.make_async_remote_copy(
            src_ref=src, dst_ref=dst, send_sem=send, recv_sem=recv,
            device_id=device, device_id_type=MESH,
        )

    ROW_ALL, ROW_A, ROW_B, ROW_C = pl.ds(0, ROWS), pl.ds(0, RA), pl.ds(RA, RB), pl.ds(RAB, RC)
    ROW_AB, ROW_BC = pl.ds(0, RAB), pl.ds(RA, RB + RC)
    COL_ALL, COL_0, COL_1 = pl.ds(0, WIDTH), pl.ds(0, HALF), pl.ds(HALF, HALF)

    gather = (
        (own + y, other + y, ROW_AB, COL_ALL, to_z),
        (own + y, own + ym, ROW_ALL, COL_ALL, to_yp),
        (own + y, own + yp, ROW_ALL, COL_ALL, to_ym),
        (other + y, other + ym, ROW_A, COL_ALL, to_yp),
        (other + y, other + yp, ROW_A, COL_ALL, to_ym),
        (own + yp, own + y2, ROW_ALL, COL_0, to_ym),
        (own + ym, own + y2, ROW_ALL, COL_1, to_yp),
        (own + yp, other + yp, ROW_B, COL_ALL, to_z),
        (own + ym, other + ym, ROW_B, COL_ALL, to_z),
        (other + yp, other + y2, ROW_A, COL_0, to_ym),
        (other + ym, other + y2, ROW_A, COL_1, to_yp),
        (own + y2, other + y2, ROW_B, COL_0, to_z),
        (own + y2, other + y2, ROW_B, COL_1, to_z),
        (own + y, other + y, ROW_C, COL_ALL, to_zc),
        (own + yp, other + yp, ROW_C, COL_ALL, to_zc),
        (own + ym, other + ym, ROW_C, COL_ALL, to_zc),
        (own + y2, other + y2, ROW_C, COL_0, to_zc),
        (own + y2, other + y2, ROW_C, COL_1, to_zc),
    )

    def ag_send(k, s):
        leaves, _, rows, cols, device = gather[k]
        ref = gb.at[s, leaves, rows, cols]
        remote(ref, ref, ag_s.at[s], ag_r.at[GATHER_GROUP[k], s], device).start()

    def arrived(ref, sem):
        remote(ref, ref, sem, sem, to_z).wait_recv()

    def left(ref, sem):
        remote(ref, ref, sem, sem, to_z).wait_send()

    def ag_wait(group, s):
        ref = (
            gb.at[s, 0, ROW_AB, :],
            gb.at[s, pl.ds(0, 2)],
            gb.at[s, pl.ds(0, 2), ROW_A, :],
            gb.at[s, 0],
            gb.at[s, pl.ds(0, 3), pl.ds(0, 112), :],
        )[group]
        arrived(ref, ag_r.at[group, s])

    HEAD_B, TAIL_C, ALL = pl.ds(0, RB), pl.ds(RB, RC), slice(None)
    reduction = (
        (other + yp, ROW_B, COL_ALL, rz1, 0, HEAD_B, to_z),
        (other + ym, ROW_B, COL_ALL, rz1, 1, HEAD_B, to_z),
        (other + y2, ROW_B, COL_ALL, rz1, 2, HEAD_B, to_z),
        (other + y2, ROW_A, COL_0, rho, 0, ALL, to_yp),
        (other + y2, ROW_A, COL_1, rho, 1, ALL, to_ym),
        (own + y2, ROW_ALL, COL_0, rhw, 0, ALL, to_yp),
        (own + y2, ROW_ALL, COL_1, rhw, 1, ALL, to_ym),
        (other + yp, ROW_A, COL_ALL, rfo, 0, ALL, to_yp),
        (other + ym, ROW_A, COL_ALL, rfo, 1, ALL, to_ym),
        (own + yp, ROW_ALL, COL_ALL, rfw, 0, ALL, to_yp),
        (own + ym, ROW_ALL, COL_ALL, rfw, 1, ALL, to_ym),
        (other + y, ROW_AB, COL_ALL, rz2, 0, ROW_AB, to_z),
        (other + yp, ROW_C, COL_ALL, rz1, 0, TAIL_C, to_zc),
        (other + ym, ROW_C, COL_ALL, rz1, 1, TAIL_C, to_zc),
        (other + y2, ROW_C, COL_ALL, rz1, 2, TAIL_C, to_zc),
        (other + y, ROW_C, COL_ALL, rz2, 0, ROW_C, to_zc),
    )

    def rs_send(k, s):
        slot, rows, cols, land, index, part, device = reduction[k]
        remote(
            p.at[s, slot, rows, cols], land.at[s, index, part, :],
            rs_s.at[s], rs_r.at[REDUCE_GROUP[k], s], device,
        ).start()

    def rs_wait(group, s):
        ref = (
            p.at[s, pl.ds(0, 3), ROW_AB, :],
            p.at[s, 0, ROW_A, :],
            p.at[s, 0],
            p.at[s, pl.ds(0, 2), ROW_A, :],
            p.at[s, pl.ds(0, 3)],
        )[group]
        arrived(ref, rs_r.at[group, s])

    def core_copy(s):
        return remote(cs.at[s], cr.at[s], c_s, c_r.at[s], to_core)

    def x_copy(s):
        return remote(ck.at[s], xr.at[s], x_s, x_r, to_x(distance(s)))

    zh_copy = remote(zs, zr, zh_s, zh_r, to_zh)
    swapped = h_v.at[pl.ds(other, 4), ROW_C, :]
    h_swap = remote(swapped, hx, sw_s.at[0], sw_r.at[0], to_zh)
    grad_swap = remote(gs, gr, sw_s.at[1], sw_r.at[1], to_zh)

    def a0(s):
        for k in (1, 2, 0, 13):
            ag_send(k, s)

    def a1(s):
        ag_wait(0, s)
        ag_send(3, s)
        ag_send(4, s)
        ag_wait(1, s)
        for k in (5, 6, 7, 8, 14, 15):
            ag_send(k, s)

    def a2(s):
        ag_wait(2, s)
        ag_send(9, s)
        ag_send(10, s)
        ag_wait(3, s)
        for k in (11, 12, 16, 17):
            ag_send(k, s)

    def a3(s):
        ag_wait(4, s)

        def weight_half(side, dst):
            cols = pl.ds(pl.multiple_of(side * HALF, HALF), HALF)

            def tile(t, carry):
                rows = pl.ds(pl.multiple_of(t * 448, 64), 448)
                block = gb[s, :, :, cols].reshape(8 * ROWS, HALF)
                product = jnp.dot(ht_v[rows, :], block, preferred_element_type=F32)
                dst[s, rows, :] = (product * scale).astype(BF16)
                return carry

            lax.fori_loop(0, 2, tile, 0)

        weight_half(1 - core, cs)
        core_copy(s).start()
        weight_half(core, ck)

        def tile(t, carry):
            rows = pl.ds(t * 4, 4)
            block = gb[s, rows].reshape(512, WIDTH)
            product = lax.dot_general(
                block, w_v[s], (((1,), (1,)), ((), ())), preferred_element_type=F32
            ).reshape(4, ROWS, FF)

            @pl.when(s == 0)
            def _():
                hg[rows] = product

            @pl.when(s > 0)
            def _():
                hg[rows] += product

            return carry

        lax.fori_loop(0, 2, tile, 0)

    def d1(s):
        core_copy(s).wait_recv()
        add_rows(ck.at[s], [cr.at[s]], FF)

        @pl.when(s < 6)
        def _():
            x_copy(s).start()

    def d2a():
        arrived(xr, x_r)

        def tile(t, carry):
            sl = pl.ds(pl.multiple_of(t * 16, 16), 16)
            total = ck[7 - zh, sl, :].astype(F32)
            for k, d in ((0, 2), (1, 2), (4, 1)):
                total += xr[k + (1 - zh) * d, sl, :].astype(F32)
            zs[sl, :] = total.astype(BF16)
            return carry

        lax.fori_loop(0, FF // 16, tile, 0)
        zh_copy.start()

    save_d = pltpu.make_async_copy(gd_v, gd_out, st_d)

    def d2b():
        zh_copy.wait_recv()

        def tile(t, carry):
            sl = pl.ds(pl.multiple_of(t * 16, 16), 16)
            total = ck[6 + zh, sl, :].astype(F32) + zr[sl, :].astype(F32)
            for k, d in ((0, 2), (1, 2), (4, 1)):
                total += xr[k + zh * d, sl, :].astype(F32)
            gd_v[sl, :] = total
            return carry

        lax.fori_loop(0, FF // 16, tile, 0)
        save_d.start()

    def r0(s):
        def tile(t, carry):
            rows = pl.ds(t * 4, 4)
            product = jnp.dot(
                h_v[rows].reshape(512, FF), w_v[s], preferred_element_type=F32
            )
            p[s, rows] = product.astype(BF16).reshape(4, ROWS, WIDTH)
            return carry

        lax.fori_loop(0, 2, tile, 0)
        for k in (0, 12, 1, 13, 2, 14, 3, 4):
            rs_send(k, s)

    def r1(s):
        rs_wait(0, s)
        for k, slot in ((2, own + y2), (0, own + yp), (1, own + ym)):
            add_rows(p.at[s, slot, ROW_BC, :], [rz1.at[s, k]], RB + RC)
            if k == 2:
                rs_send(5, s)
                rs_send(6, s)

    def r2(s):
        rs_wait(1, s)
        add_rows(p.at[s, other + yp, ROW_A, COL_0], [rho.at[s, 0]], RA)
        rs_send(7, s)
        add_rows(p.at[s, other + ym, ROW_A, COL_1], [rho.at[s, 1]], RA)
        rs_send(8, s)
        rs_wait(2, s)
        add_rows(p.at[s, own + yp, ROW_ALL, COL_0], [rhw.at[s, 0]], ROWS)
        rs_send(9, s)
        add_rows(p.at[s, own + ym, ROW_ALL, COL_1], [rhw.at[s, 1]], ROWS)
        rs_send(10, s)

    def r3(s):
        rs_send(15, s)
        rs_wait(3, s)
        add_rows(p.at[s, other + y, ROW_A, :], [rfo.at[s, 0], rfo.at[s, 1]], RA)
        rs_send(11, s)

    def save_f(s):
        return pltpu.make_async_copy(p.at[s, te], f_out.at[:, column(s)], st_f)

    def r4(s):
        rs_wait(4, s)
        add_rows(p.at[s, te], [rfw.at[s, 0], rfw.at[s, 1], rz2.at[s, 0]], ROWS)
        save_f(s).start()

    def save_e(e, which):
        first = jnp.where(e < 2, own, other) + (e % 2) * 2
        rows = pl.ds(pl.multiple_of(first * ROWS, 2 * ROWS), 2 * ROWS)
        src, dst = ((gate_v, gg_out), (up_v, gu_out))[which]
        return pltpu.make_async_copy(src.at[rows, :], dst.at[rows, :], st_e.at[which])

    def e0(e):
        first = jnp.where(e < 2, own, other) + (e % 2) * 2

        def tile(t, carry):
            slot = first + t // 8
            row = pl.multiple_of((t % 8) * 16, 16)
            sl = pl.ds(pl.multiple_of(slot * ROWS + row, 16), 16)
            g = gate_v[sl, :].astype(F32)
            u = up_v[sl, :].astype(F32)
            grad = hg[slot, pl.ds(row, 16), :]
            s = jax.nn.sigmoid(g)
            gate_v[sl, :] = (grad * u * s * (1.0 + g * (1.0 - s))).astype(BF16)
            up_v[sl, :] = (grad * (g * s)).astype(BF16)
            return carry

        lax.fori_loop(0, 16, tile, 0)
        save_e(e, 0).start()
        save_e(e, 1).start()

    def swap_tiles(f):
        def tile(t, carry):
            row = pl.multiple_of((t % 3) * 16, 16)
            f(t // 3, pl.ds(row, 16), pl.ds(RAB + row, 16))
            return carry

        lax.fori_loop(0, 4 * (RC // 16), tile, 0)

    def gx():
        def move(k, part, row):
            gs[k, part, :] = hg[other + k, row, :].astype(BF16)

        swap_tiles(move)
        grad_swap.start()

    def gr_stage():
        grad_swap.wait_recv()

        def move(k, part, row):
            hg[other + k, row, :] = gr[k, part, :].astype(F32)

        swap_tiles(move)

    def hidden_rows(slot, row, count):
        def tile(t, carry):
            start = pl.multiple_of(row + t * 16, 16)
            sl = pl.ds(pl.multiple_of(slot * ROWS + start, 16), 16)
            g = gate_v[sl, :].astype(F32)
            u = up_v[sl, :].astype(F32)
            h_v[slot, pl.ds(start, 16), :] = (g * jax.nn.sigmoid(g) * u).astype(BF16)
            return carry

        lax.fori_loop(0, count // 16, tile, 0)

    def hx_stage():
        pltpu.make_async_copy(w_v, w_v, ld_w).wait()
        h_swap.wait_send()
        h_swap.wait_recv()

        def move(k, part, row):
            h_v[other + k, row, :] = hx[k, part, :]

        swap_tiles(move)

        def transpose_tile(t, carry):
            ht_v[:, pl.ds(pl.multiple_of(t * ROWS, ROWS), ROWS)] = h_v[t].T
            return carry

        lax.fori_loop(0, 8, transpose_tile, 0)

    pltpu.make_async_copy(gb.at[:, te], gb.at[:, te], ld_g).wait()
    each(LOOKAHEAD, a0)
    load_gate.wait()
    load_up.wait()

    each(4, lambda k: hidden_rows(other + k, RAB, RC))
    h_swap.start()
    each(4, lambda k: hidden_rows(own + k, 0, ROWS))
    each(4, lambda k: hidden_rows(other + k, 0, RAB))

    def iteration(i, carry):
        def stage(name, f, count=STEPS):
            s = i - OFF[name]

            @pl.when((s >= 0) & (s < count))
            def _():
                f(s)

        @pl.when(i + LOOKAHEAD < STEPS)
        def _():
            a0(i + LOOKAHEAD)

        stage("A1", a1)
        stage("A2", a2)
        stage("HX", lambda s: hx_stage(), 1)
        stage("R0", r0)
        stage("R1", r1)
        stage("R2", r2)
        stage("R3", r3)
        stage("A3", a3)
        stage("GX", lambda s: gx(), 1)
        stage("D1", d1)
        stage("D2A", lambda s: d2a(), 1)
        stage("R4", r4)
        stage("GR", lambda s: gr_stage(), 1)
        stage("E", e0, 4)
        stage("D2B", lambda s: d2b(), 1)
        return carry

    lax.fori_loop(0, ITERS, iteration, 0)

    def finish(s):
        left(gb.at[s, pl.ds(0, 7)], ag_s.at[s])
        left(p.at[s, pl.ds(0, 7)], rs_s.at[s])

    each(STEPS, finish)
    left(cs, c_s)
    left(xr, x_s)
    zh_copy.wait_send()
    grad_swap.wait_send()
    pltpu.make_async_copy(p.at[:, te], p.at[:, te], st_f).wait()
    pltpu.make_async_copy(gate_v, gg_out, st_e.at[0]).wait()
    pltpu.make_async_copy(up_v, gu_out, st_e.at[1]).wait()
    save_d.wait()


PIECES = 4


def settle_kernel(a0, a1, a2, a3, b0, b1, b2, b3, v0, v1, v2, v3, load_sem, save_sem):
    pieces = []
    for k, (src, mid, dst) in enumerate(((a1, v1, b1), (a2, v2, b2), (a0, v0, b0), (a3, v3, b3))):
        count = src.shape[0] // PIECES
        for part in range(PIECES):
            rows = pl.ds(part * count, count)
            n = k * PIECES + part
            pieces.append((
                pltpu.make_async_copy(src.at[rows, :], mid.at[rows, :], load_sem.at[n]),
                pltpu.make_async_copy(mid.at[rows, :], dst.at[rows, :], save_sem.at[n]),
            ))
    for load, _ in pieces:
        load.start()
    for load, save in pieces:
        load.wait()
        save.start()
    for _, save in pieces:
        save.wait()


def settle(outs):
    anywhere = pl.BlockSpec(memory_space=pl.ANY)
    return pl.pallas_call(
        settle_kernel,
        out_shape=tuple(jax.ShapeDtypeStruct(o.shape, o.dtype) for o in outs),
        in_specs=[anywhere] * 4,
        out_specs=[anywhere] * 4,
        scratch_shapes=[pltpu.VMEM(o.shape, o.dtype) for o in outs]
        + [pltpu.SemaphoreType.DMA((4 * PIECES,))] * 2,
        compiler_params=pltpu.CompilerParams(vmem_limit_bytes=60 * 1024 * 1024),
        cost_estimate=pl.CostEstimate(flops=0, bytes_accessed=11_000_000, transcendentals=0),
    )(*outs)


def body(gate_pre, up_pre, down_weight, grad_out):
    replica_rows, ff = gate_pre.shape
    rows, width = grad_out.shape
    scale = 1.0 / math.sqrt(replica_rows * lax.axis_size("dp"))
    vmem, dma = pltpu.VMEM, pltpu.SemaphoreType.DMA
    anywhere = pl.BlockSpec(memory_space=pl.ANY)
    outs = pl.pallas_call(
        functools.partial(kernel, scale),
        out_shape=(
            jax.ShapeDtypeStruct((rows, width), BF16),
            jax.ShapeDtypeStruct((replica_rows, ff), BF16),
            jax.ShapeDtypeStruct((replica_rows, ff), BF16),
            jax.ShapeDtypeStruct((ff, width // 16), F32),
        ),
        in_specs=[anywhere] * 4,
        out_specs=[anywhere] * 4,
        scratch_shapes=[
            vmem((replica_rows, ff), BF16),
            vmem((replica_rows, ff), BF16),
            vmem((STEPS, ff, WIDTH), BF16),
            vmem((8, ROWS, ff), BF16),
            vmem((ff, replica_rows), BF16),
            vmem((STEPS, 8, ROWS, WIDTH), BF16),
            vmem((STEPS, 8, ROWS, WIDTH), BF16),
            vmem((8, ROWS, ff), F32),
            vmem((STEPS, 3, RB + RC, WIDTH), BF16),
            vmem((STEPS, 2, RA, HALF), BF16),
            vmem((STEPS, 2, ROWS, HALF), BF16),
            vmem((STEPS, 2, RA, WIDTH), BF16),
            vmem((STEPS, 2, ROWS, WIDTH), BF16),
            vmem((STEPS, 1, ROWS, WIDTH), BF16),
            vmem((4, RC, ff), BF16),
            vmem((4, RC, ff), BF16),
            vmem((4, RC, ff), BF16),
            vmem((STEPS, ff, HALF), BF16),
            vmem((STEPS, ff, HALF), BF16),
            vmem((STEPS, ff, HALF), BF16),
            vmem((6, ff, HALF), BF16),
            vmem((ff, HALF), BF16),
            vmem((ff, HALF), BF16),
            vmem((ff, HALF), F32),
            dma((STEPS,)), dma((5, STEPS)),
            dma((STEPS,)), dma((5, STEPS)),
            dma, dma((STEPS,)),
            dma, dma,
            dma, dma,
            dma((2,)), dma((2,)),
            dma, dma, dma((2,)),
            dma, dma((2,)), dma,
        ],
        compiler_params=pltpu.CompilerParams(
            collective_id=0, has_side_effects=True, vmem_limit_bytes=60 * 1024 * 1024
        ),
        cost_estimate=pl.CostEstimate(
            flops=6 * replica_rows * ff * width, bytes_accessed=20_000_000, transcendentals=2_000_000
        ),
    )(gate_pre, up_pre, down_weight, grad_out)
    return settle(outs)


def solution(mesh):
    return jax.shard_map(
        body,
        mesh=mesh,
        in_specs=(
            P("dp", "tensor"),
            P("dp", "tensor"),
            P("tensor", None),
            P(("dp", "tensor"), None),
        ),
        out_specs=(
            P(("dp", "tensor"), None),
            P("dp", "tensor"),
            P("dp", "tensor"),
            P("tensor", "dp"),
        ),
        check_vma=False,
    )
```

```python
import functools
import math

import jax
import jax.numpy as jnp
from jax import lax
from jax.experimental import pallas as pl
from jax.experimental.pallas import tpu as pltpu
from jax.sharding import PartitionSpec as P

MESH = pl.DeviceIdType.MESH
F32 = jnp.float32
BF16 = jnp.bfloat16

GATHER_GROUP = (0, 1, 1, 2, 2, 3, 3) + (4,) * 11
REDUCE_GROUP = (0, 0, 0, 1, 1, 2, 2, 3, 3, 4, 4, 4, 0, 0, 0, 4)

STEPS = 8
WIDTH = 512
HALF = 256
ROWS = 128
RA = 48
RB = 32
RC = 48
RAB = RA + RB
FF = 896

LOOKAHEAD = 3
OFF = dict(A1=0, HX=1, A2=1, A3=2, D1=3, R0=2, R1=4, R2=6, R3=8, R4=10, GX=9, GR=11, E=10, D2A=12, D2B=17)
ITERS = 18


def add_rows(dst, srcs, rows):
    def step(t, carry):
        sl = pl.ds(pl.multiple_of(t * 16, 16), 16)
        total = dst[sl, :].astype(F32)
        for src in srcs:
            total += src[sl, :].astype(F32)
        dst[sl, :] = total.astype(dst.dtype)
        return carry

    lax.fori_loop(0, rows // 16, step, 0)


def kernel(
    scale,
    gate_hbm, up_hbm, w_hbm, g_hbm,
    f_out, gg_out, gu_out, gd_out,
    gate_v, up_v, w_v, h_v, ht_v, gb, p, hg,
    rz1, rho, rhw, rfo, rfw, rz2,
    hx, gs, gr,
    cs, ck, cr, xr, zs, zr, gd_v,
    ag_s, ag_r, rs_s, rs_r, c_s, c_r, x_s, x_r, zh_s, zh_r, sw_s, sw_r,
    ld_g, ld_w, ld_a, st_f, st_e, st_d,
):
    dp = lax.axis_index("dp")
    te = lax.axis_index("tensor")
    x, zh, core = dp // 4, (dp // 2) % 2, dp % 2
    z, y = te // 4, te % 4
    yp, ym, y2 = (y + 1) % 4, (y + 3) % 4, (y + 2) % 4
    zo = 1 - z
    own, other = z * 4, zo * 4
    to_yp, to_ym, to_z = (dp, own + yp), (dp, own + ym), (dp, other + y)
    to_core = (x * 4 + zh * 2 + (1 - core), te)
    to_zh = (x * 4 + (1 - zh) * 2 + core, te)
    to_zc = (x * 4 + (1 - zh) * 2 + core, other + y)

    def to_x(d):
        return (((x + d) % 4) * 4 + zh * 2 + core, te)

    def distance(s):
        return jnp.where(s < 4, 1 + 2 * (s % 2), jnp.where(s < 6, 2, 0))

    def column(s):
        j = 2 * ((x + distance(s)) % 4) + jnp.where(s < 4, s // 2, s % 2)
        return pl.ds(pl.multiple_of(j * WIDTH, WIDTH), WIDTH)

    def load_g(s):
        return pltpu.make_async_copy(g_hbm.at[:, column(s)], gb.at[s, te], ld_g)

    def load_w(s):
        return pltpu.make_async_copy(w_hbm.at[:, column(s)], w_v.at[s], ld_w)

    load_gate = pltpu.make_async_copy(gate_hbm, gate_v, ld_a.at[0])
    load_up = pltpu.make_async_copy(up_hbm, up_v, ld_a.at[1])

    def each(n, f):
        def step(s, carry):
            f(s)
            return carry

        lax.fori_loop(0, n, step, 0)

    each(STEPS, lambda s: load_g(s).start())
    load_gate.start()
    load_up.start()
    each(STEPS, lambda s: load_w(s).start())

    barrier = pltpu.get_barrier_semaphore()
    for device in (to_yp, to_ym, to_z, to_zc, to_core, to_zh, to_x(1), to_x(2), to_x(3)):
        pl.semaphore_signal(barrier, inc=1, device_id=device, device_id_type=MESH)
    pl.semaphore_wait(barrier, 9)

    def remote(src, dst, send, recv, device):
        return pltpu.make_async_remote_copy(
            src_ref=src, dst_ref=dst, send_sem=send, recv_sem=recv,
            device_id=device, device_id_type=MESH,
        )

    ROW_ALL, ROW_A, ROW_B, ROW_C = pl.ds(0, ROWS), pl.ds(0, RA), pl.ds(RA, RB), pl.ds(RAB, RC)
    ROW_AB, ROW_BC = pl.ds(0, RAB), pl.ds(RA, RB + RC)
    COL_ALL, COL_0, COL_1 = pl.ds(0, WIDTH), pl.ds(0, HALF), pl.ds(HALF, HALF)

    gather = (
        (own + y, other + y, ROW_AB, COL_ALL, to_z),
        (own + y, own + ym, ROW_ALL, COL_ALL, to_yp),
        (own + y, own + yp, ROW_ALL, COL_ALL, to_ym),
        (other + y, other + ym, ROW_A, COL_ALL, to_yp),
        (other + y, other + yp, ROW_A, COL_ALL, to_ym),
        (own + yp, own + y2, ROW_ALL, COL_0, to_ym),
        (own + ym, own + y2, ROW_ALL, COL_1, to_yp),
        (own + yp, other + yp, ROW_B, COL_ALL, to_z),
        (own + ym, other + ym, ROW_B, COL_ALL, to_z),
        (other + yp, other + y2, ROW_A, COL_0, to_ym),
        (other + ym, other + y2, ROW_A, COL_1, to_yp),
        (own + y2, other + y2, ROW_B, COL_0, to_z),
        (own + y2, other + y2, ROW_B, COL_1, to_z),
        (own + y, other + y, ROW_C, COL_ALL, to_zc),
        (own + yp, other + yp, ROW_C, COL_ALL, to_zc),
        (own + ym, other + ym, ROW_C, COL_ALL, to_zc),
        (own + y2, other + y2, ROW_C, COL_0, to_zc),
        (own + y2, other + y2, ROW_C, COL_1, to_zc),
    )

    def ag_send(k, s):
        leaves, _, rows, cols, device = gather[k]
        ref = gb.at[s, leaves, rows, cols]
        remote(ref, ref, ag_s.at[s], ag_r.at[GATHER_GROUP[k], s], device).start()

    def arrived(ref, sem):
        remote(ref, ref, sem, sem, to_z).wait_recv()

    def left(ref, sem):
        remote(ref, ref, sem, sem, to_z).wait_send()

    def ag_wait(group, s):
        ref = (
            gb.at[s, 0, ROW_AB, :],
            gb.at[s, pl.ds(0, 2)],
            gb.at[s, pl.ds(0, 2), ROW_A, :],
            gb.at[s, 0],
            gb.at[s, pl.ds(0, 3), pl.ds(0, 112), :],
        )[group]
        arrived(ref, ag_r.at[group, s])

    HEAD_B, TAIL_C, ALL = pl.ds(0, RB), pl.ds(RB, RC), slice(None)
    reduction = (
        (other + yp, ROW_B, COL_ALL, rz1, 0, HEAD_B, to_z),
        (other + ym, ROW_B, COL_ALL, rz1, 1, HEAD_B, to_z),
        (other + y2, ROW_B, COL_ALL, rz1, 2, HEAD_B, to_z),
        (other + y2, ROW_A, COL_0, rho, 0, ALL, to_yp),
        (other + y2, ROW_A, COL_1, rho, 1, ALL, to_ym),
        (own + y2, ROW_ALL, COL_0, rhw, 0, ALL, to_yp),
        (own + y2, ROW_ALL, COL_1, rhw, 1, ALL, to_ym),
        (other + yp, ROW_A, COL_ALL, rfo, 0, ALL, to_yp),
        (other + ym, ROW_A, COL_ALL, rfo, 1, ALL, to_ym),
        (own + yp, ROW_ALL, COL_ALL, rfw, 0, ALL, to_yp),
        (own + ym, ROW_ALL, COL_ALL, rfw, 1, ALL, to_ym),
        (other + y, ROW_AB, COL_ALL, rz2, 0, ROW_AB, to_z),
        (other + yp, ROW_C, COL_ALL, rz1, 0, TAIL_C, to_zc),
        (other + ym, ROW_C, COL_ALL, rz1, 1, TAIL_C, to_zc),
        (other + y2, ROW_C, COL_ALL, rz1, 2, TAIL_C, to_zc),
        (other + y, ROW_C, COL_ALL, rz2, 0, ROW_C, to_zc),
    )

    def rs_send(k, s):
        slot, rows, cols, land, index, part, device = reduction[k]
        remote(
            p.at[s, slot, rows, cols], land.at[s, index, part, :],
            rs_s.at[s], rs_r.at[REDUCE_GROUP[k], s], device,
        ).start()

    def rs_wait(group, s):
        ref = (
            p.at[s, pl.ds(0, 3), ROW_AB, :],
            p.at[s, 0, ROW_A, :],
            p.at[s, 0],
            p.at[s, pl.ds(0, 2), ROW_A, :],
            p.at[s, pl.ds(0, 3)],
        )[group]
        arrived(ref, rs_r.at[group, s])

    def core_copy(s):
        return remote(cs.at[s], cr.at[s], c_s, c_r.at[s], to_core)

    def x_copy(s):
        return remote(ck.at[s], xr.at[s], x_s, x_r, to_x(distance(s)))

    zh_copy = remote(zs, zr, zh_s, zh_r, to_zh)
    swapped = h_v.at[pl.ds(other, 4), ROW_C, :]
    h_swap = remote(swapped, hx, sw_s.at[0], sw_r.at[0], to_zh)
    grad_swap = remote(gs, gr, sw_s.at[1], sw_r.at[1], to_zh)

    def a0(s):
        for k in (1, 2, 0, 13):
            ag_send(k, s)

    def a1(s):
        ag_wait(0, s)
        ag_send(3, s)
        ag_send(4, s)
        ag_wait(1, s)
        for k in (5, 6, 7, 8, 14, 15):
            ag_send(k, s)

    def a2(s):
        ag_wait(2, s)
        ag_send(9, s)
        ag_send(10, s)
        ag_wait(3, s)
        for k in (11, 12, 16, 17):
            ag_send(k, s)

    def a3(s):
        ag_wait(4, s)

        def weight_half(side, dst):
            cols = pl.ds(pl.multiple_of(side * HALF, HALF), HALF)

            def tile(t, carry):
                rows = pl.ds(pl.multiple_of(t * 448, 64), 448)
                block = gb[s, :, :, cols].reshape(8 * ROWS, HALF)
                product = jnp.dot(ht_v[rows, :], block, preferred_element_type=F32)
                dst[s, rows, :] = (product * scale).astype(BF16)
                return carry

            lax.fori_loop(0, 2, tile, 0)

        weight_half(1 - core, cs)
        core_copy(s).start()
        weight_half(core, ck)

        def tile(t, carry):
            rows = pl.ds(t * 4, 4)
            block = gb[s, rows].reshape(512, WIDTH)
            product = lax.dot_general(
                block, w_v[s], (((1,), (1,)), ((), ())), preferred_element_type=F32
            ).reshape(4, ROWS, FF)

            @pl.when(s == 0)
            def _():
                hg[rows] = product

            @pl.when(s > 0)
            def _():
                hg[rows] += product

            return carry

        lax.fori_loop(0, 2, tile, 0)

    def d1(s):
        core_copy(s).wait_recv()
        add_rows(ck.at[s], [cr.at[s]], FF)

        @pl.when(s < 6)
        def _():
            x_copy(s).start()

    def d2a():
        arrived(xr, x_r)

        def tile(t, carry):
            sl = pl.ds(pl.multiple_of(t * 16, 16), 16)
            total = ck[7 - zh, sl, :].astype(F32)
            for k, d in ((0, 2), (1, 2), (4, 1)):
                total += xr[k + (1 - zh) * d, sl, :].astype(F32)
            zs[sl, :] = total.astype(BF16)
            return carry

        lax.fori_loop(0, FF // 16, tile, 0)
        zh_copy.start()

    save_d = pltpu.make_async_copy(gd_v, gd_out, st_d)

    def d2b():
        zh_copy.wait_recv()

        def tile(t, carry):
            sl = pl.ds(pl.multiple_of(t * 16, 16), 16)
            total = ck[6 + zh, sl, :].astype(F32) + zr[sl, :].astype(F32)
            for k, d in ((0, 2), (1, 2), (4, 1)):
                total += xr[k + zh * d, sl, :].astype(F32)
            gd_v[sl, :] = total
            return carry

        lax.fori_loop(0, FF // 16, tile, 0)
        save_d.start()

    def r0(s):
        def tile(t, carry):
            rows = pl.ds(t * 4, 4)
            product = jnp.dot(
                h_v[rows].reshape(512, FF), w_v[s], preferred_element_type=F32
            )
            p[s, rows] = product.astype(BF16).reshape(4, ROWS, WIDTH)
            return carry

        lax.fori_loop(0, 2, tile, 0)
        for k in (0, 12, 1, 13, 2, 14, 3, 4):
            rs_send(k, s)

    def r1(s):
        rs_wait(0, s)
        for k, slot in ((2, own + y2), (0, own + yp), (1, own + ym)):
            add_rows(p.at[s, slot, ROW_BC, :], [rz1.at[s, k]], RB + RC)
            if k == 2:
                rs_send(5, s)
                rs_send(6, s)

    def r2(s):
        rs_wait(1, s)
        add_rows(p.at[s, other + yp, ROW_A, COL_0], [rho.at[s, 0]], RA)
        rs_send(7, s)
        add_rows(p.at[s, other + ym, ROW_A, COL_1], [rho.at[s, 1]], RA)
        rs_send(8, s)
        rs_wait(2, s)
        add_rows(p.at[s, own + yp, ROW_ALL, COL_0], [rhw.at[s, 0]], ROWS)
        rs_send(9, s)
        add_rows(p.at[s, own + ym, ROW_ALL, COL_1], [rhw.at[s, 1]], ROWS)
        rs_send(10, s)

    def r3(s):
        rs_send(15, s)
        rs_wait(3, s)
        add_rows(p.at[s, other + y, ROW_A, :], [rfo.at[s, 0], rfo.at[s, 1]], RA)
        rs_send(11, s)

    def save_f(s):
        return pltpu.make_async_copy(p.at[s, te], f_out.at[:, column(s)], st_f)

    def r4(s):
        rs_wait(4, s)
        add_rows(p.at[s, te], [rfw.at[s, 0], rfw.at[s, 1], rz2.at[s, 0]], ROWS)
        save_f(s).start()

    def save_e(e, which):
        first = jnp.where(e < 2, own, other) + (e % 2) * 2
        rows = pl.ds(pl.multiple_of(first * ROWS, 2 * ROWS), 2 * ROWS)
        src, dst = ((gate_v, gg_out), (up_v, gu_out))[which]
        return pltpu.make_async_copy(src.at[rows, :], dst.at[rows, :], st_e.at[which])

    def e0(e):
        first = jnp.where(e < 2, own, other) + (e % 2) * 2

        def tile(t, carry):
            slot = first + t // 8
            row = pl.multiple_of((t % 8) * 16, 16)
            sl = pl.ds(pl.multiple_of(slot * ROWS + row, 16), 16)
            g = gate_v[sl, :].astype(F32)
            u = up_v[sl, :].astype(F32)
            grad = hg[slot, pl.ds(row, 16), :]
            s = jax.nn.sigmoid(g)
            gate_v[sl, :] = (grad * u * s * (1.0 + g * (1.0 - s))).astype(BF16)
            up_v[sl, :] = (grad * (g * s)).astype(BF16)
            return carry

        lax.fori_loop(0, 16, tile, 0)
        save_e(e, 0).start()
        save_e(e, 1).start()

    def swap_tiles(f):
        def tile(t, carry):
            row = pl.multiple_of((t % 3) * 16, 16)
            f(t // 3, pl.ds(row, 16), pl.ds(RAB + row, 16))
            return carry

        lax.fori_loop(0, 4 * (RC // 16), tile, 0)

    def gx():
        def move(k, part, row):
            gs[k, part, :] = hg[other + k, row, :].astype(BF16)

        swap_tiles(move)
        grad_swap.start()

    def gr_stage():
        grad_swap.wait_recv()

        def move(k, part, row):
            hg[other + k, row, :] = gr[k, part, :].astype(F32)

        swap_tiles(move)

    def hidden_rows(slot, row, count):
        def tile(t, carry):
            start = pl.multiple_of(row + t * 16, 16)
            sl = pl.ds(pl.multiple_of(slot * ROWS + start, 16), 16)
            g = gate_v[sl, :].astype(F32)
            u = up_v[sl, :].astype(F32)
            h_v[slot, pl.ds(start, 16), :] = (g * jax.nn.sigmoid(g) * u).astype(BF16)
            return carry

        lax.fori_loop(0, count // 16, tile, 0)

    def hx_stage():
        pltpu.make_async_copy(w_v, w_v, ld_w).wait()
        h_swap.wait_send()
        h_swap.wait_recv()

        def move(k, part, row):
            h_v[other + k, row, :] = hx[k, part, :]

        swap_tiles(move)

        def transpose_tile(t, carry):
            ht_v[:, pl.ds(pl.multiple_of(t * ROWS, ROWS), ROWS)] = h_v[t].T
            return carry

        lax.fori_loop(0, 8, transpose_tile, 0)

    pltpu.make_async_copy(gb.at[:, te], gb.at[:, te], ld_g).wait()
    each(LOOKAHEAD, a0)
    load_gate.wait()
    load_up.wait()

    each(4, lambda k: hidden_rows(other + k, RAB, RC))
    h_swap.start()
    each(4, lambda k: hidden_rows(own + k, 0, ROWS))
    each(4, lambda k: hidden_rows(other + k, 0, RAB))

    def iteration(i, carry):
        def stage(name, f, count=STEPS):
            s = i - OFF[name]

            @pl.when((s >= 0) & (s < count))
            def _():
                f(s)

        stage("A1", a1)
        stage("A2", a2)

        @pl.when(i + LOOKAHEAD < STEPS)
        def _():
            a0(i + LOOKAHEAD)

        stage("HX", lambda s: hx_stage(), 1)
        stage("R0", r0)
        stage("R1", r1)
        stage("R2", r2)
        stage("R3", r3)
        stage("A3", a3)
        stage("GX", lambda s: gx(), 1)
        stage("D1", d1)
        stage("D2A", lambda s: d2a(), 1)
        stage("R4", r4)
        stage("GR", lambda s: gr_stage(), 1)
        stage("E", e0, 4)
        stage("D2B", lambda s: d2b(), 1)
        return carry

    lax.fori_loop(0, ITERS, iteration, 0)

    def finish(s):
        left(gb.at[s, pl.ds(0, 7)], ag_s.at[s])
        left(p.at[s, pl.ds(0, 7)], rs_s.at[s])

    each(STEPS, finish)
    left(cs, c_s)
    left(xr, x_s)
    zh_copy.wait_send()
    grad_swap.wait_send()
    pltpu.make_async_copy(p.at[:, te], p.at[:, te], st_f).wait()
    pltpu.make_async_copy(gate_v, gg_out, st_e.at[0]).wait()
    pltpu.make_async_copy(up_v, gu_out, st_e.at[1]).wait()
    save_d.wait()


PIECES = 2


def settle_kernel(a0, a1, a2, a3, b0, b1, b2, b3, v0, v1, v2, v3, load_sem, save_sem):
    pieces = []
    for k, (src, mid, dst) in enumerate(((a1, v1, b1), (a2, v2, b2), (a0, v0, b0), (a3, v3, b3))):
        count = src.shape[0] // PIECES
        for part in range(PIECES):
            rows = pl.ds(part * count, count)
            n = k * PIECES + part
            pieces.append((
                pltpu.make_async_copy(src.at[rows, :], mid.at[rows, :], load_sem.at[n]),
                pltpu.make_async_copy(mid.at[rows, :], dst.at[rows, :], save_sem.at[n]),
            ))
    for load, _ in pieces:
        load.start()
    for load, save in pieces:
        load.wait()
        save.start()
    for _, save in pieces:
        save.wait()


def settle(outs):
    anywhere = pl.BlockSpec(memory_space=pl.ANY)
    return pl.pallas_call(
        settle_kernel,
        out_shape=tuple(jax.ShapeDtypeStruct(o.shape, o.dtype) for o in outs),
        in_specs=[anywhere] * 4,
        out_specs=[anywhere] * 4,
        scratch_shapes=[pltpu.VMEM(o.shape, o.dtype) for o in outs]
        + [pltpu.SemaphoreType.DMA((4 * PIECES,))] * 2,
        compiler_params=pltpu.CompilerParams(vmem_limit_bytes=60 * 1024 * 1024),
        cost_estimate=pl.CostEstimate(flops=0, bytes_accessed=11_000_000, transcendentals=0),
    )(*outs)


def body(gate_pre, up_pre, down_weight, grad_out):
    replica_rows, ff = gate_pre.shape
    rows, width = grad_out.shape
    scale = 1.0 / math.sqrt(replica_rows * lax.axis_size("dp"))
    vmem, dma = pltpu.VMEM, pltpu.SemaphoreType.DMA
    anywhere = pl.BlockSpec(memory_space=pl.ANY)
    outs = pl.pallas_call(
        functools.partial(kernel, scale),
        out_shape=(
            jax.ShapeDtypeStruct((rows, width), BF16),
            jax.ShapeDtypeStruct((replica_rows, ff), BF16),
            jax.ShapeDtypeStruct((replica_rows, ff), BF16),
            jax.ShapeDtypeStruct((ff, width // 16), F32),
        ),
        in_specs=[anywhere] * 4,
        out_specs=[anywhere] * 4,
        scratch_shapes=[
            vmem((replica_rows, ff), BF16),
            vmem((replica_rows, ff), BF16),
            vmem((STEPS, ff, WIDTH), BF16),
            vmem((8, ROWS, ff), BF16),
            vmem((ff, replica_rows), BF16),
            vmem((STEPS, 8, ROWS, WIDTH), BF16),
            vmem((STEPS, 8, ROWS, WIDTH), BF16),
            vmem((8, ROWS, ff), F32),
            vmem((STEPS, 3, RB + RC, WIDTH), BF16),
            vmem((STEPS, 2, RA, HALF), BF16),
            vmem((STEPS, 2, ROWS, HALF), BF16),
            vmem((STEPS, 2, RA, WIDTH), BF16),
            vmem((STEPS, 2, ROWS, WIDTH), BF16),
            vmem((STEPS, 1, ROWS, WIDTH), BF16),
            vmem((4, RC, ff), BF16),
            vmem((4, RC, ff), BF16),
            vmem((4, RC, ff), BF16),
            vmem((STEPS, ff, HALF), BF16),
            vmem((STEPS, ff, HALF), BF16),
            vmem((STEPS, ff, HALF), BF16),
            vmem((6, ff, HALF), BF16),
            vmem((ff, HALF), BF16),
            vmem((ff, HALF), BF16),
            vmem((ff, HALF), F32),
            dma((STEPS,)), dma((5, STEPS)),
            dma((STEPS,)), dma((5, STEPS)),
            dma, dma((STEPS,)),
            dma, dma,
            dma, dma,
            dma((2,)), dma((2,)),
            dma, dma, dma((2,)),
            dma, dma((2,)), dma,
        ],
        compiler_params=pltpu.CompilerParams(
            collective_id=0, has_side_effects=True, vmem_limit_bytes=60 * 1024 * 1024
        ),
        cost_estimate=pl.CostEstimate(
            flops=6 * replica_rows * ff * width, bytes_accessed=20_000_000, transcendentals=2_000_000
        ),
    )(gate_pre, up_pre, down_weight, grad_out)
    return settle(outs)


def solution(mesh):
    return jax.shard_map(
        body,
        mesh=mesh,
        in_specs=(
            P("dp", "tensor"),
            P("dp", "tensor"),
            P("tensor", None),
            P(("dp", "tensor"), None),
        ),
        out_specs=(
            P(("dp", "tensor"), None),
            P("dp", "tensor"),
            P("dp", "tensor"),
            P("tensor", "dp"),
        ),
        check_vma=False,
    )
```

```python
import functools
import math

import jax
import jax.numpy as jnp
from jax import lax
from jax.experimental import pallas as pl
from jax.experimental.pallas import tpu as pltpu
from jax.sharding import PartitionSpec as P

MESH = pl.DeviceIdType.MESH
F32 = jnp.float32
BF16 = jnp.bfloat16

GATHER_GROUP = (0, 1, 1, 2, 2, 3, 3) + (4,) * 11
REDUCE_GROUP = (0, 0, 0, 1, 1, 2, 2, 3, 3, 4, 4, 4, 0, 0, 0, 4)

STEPS = 8
WIDTH = 512
HALF = 256
ROWS = 128
RA = 48
RB = 32
RC = 48
RAB = RA + RB
FF = 896

LOOKAHEAD = 3
OFF = dict(A1=0, HX=1, A2=1, A3=2, D1=3, R0=2, R1=4, R2=6, R3=8, R4=10, GX=9, GR=11, E=10, D2A=12, D2B=17)
ITERS = 18


def add_rows(dst, srcs, rows):
    def step(t, carry):
        sl = pl.ds(pl.multiple_of(t * 16, 16), 16)
        total = dst[sl, :].astype(F32)
        for src in srcs:
            total += src[sl, :].astype(F32)
        dst[sl, :] = total.astype(dst.dtype)
        return carry

    lax.fori_loop(0, rows // 16, step, 0)


def kernel(
    scale,
    gate_hbm, up_hbm, w_hbm, g_hbm,
    f_out, gg_out, gu_out, gd_out,
    gate_v, up_v, w_v, h_v, ht_v, gb, p, hg,
    rz1, rho, rhw, rfo, rfw, rz2,
    hx, gs, gr,
    cs, ck, cr, xr, zs, zr, gd_v,
    ag_s, ag_r, rs_s, rs_r, c_s, c_r, x_s, x_r, zh_s, zh_r, sw_s, sw_r,
    ld_g, ld_w, ld_a, st_f, st_e, st_d,
):
    dp = lax.axis_index("dp")
    te = lax.axis_index("tensor")
    x, zh, core = dp // 4, (dp // 2) % 2, dp % 2
    z, y = te // 4, te % 4
    yp, ym, y2 = (y + 1) % 4, (y + 3) % 4, (y + 2) % 4
    zo = 1 - z
    own, other = z * 4, zo * 4
    to_yp, to_ym, to_z = (dp, own + yp), (dp, own + ym), (dp, other + y)
    to_core = (x * 4 + zh * 2 + (1 - core), te)
    to_zh = (x * 4 + (1 - zh) * 2 + core, te)
    to_zc = (x * 4 + (1 - zh) * 2 + core, other + y)

    def to_x(d):
        return (((x + d) % 4) * 4 + zh * 2 + core, te)

    def distance(s):
        return jnp.where(s < 4, 1 + 2 * (s % 2), jnp.where(s < 6, 2, 0))

    def column(s):
        j = 2 * ((x + distance(s)) % 4) + jnp.where(s < 4, s // 2, s % 2)
        return pl.ds(pl.multiple_of(j * WIDTH, WIDTH), WIDTH)

    def load_g(s):
        return pltpu.make_async_copy(g_hbm.at[:, column(s)], gb.at[s, te], ld_g)

    def load_w(s):
        return pltpu.make_async_copy(w_hbm.at[:, column(s)], w_v.at[s], ld_w)

    load_gate = pltpu.make_async_copy(gate_hbm, gate_v, ld_a.at[0])
    load_up = pltpu.make_async_copy(up_hbm, up_v, ld_a.at[1])

    def each(n, f):
        def step(s, carry):
            f(s)
            return carry

        lax.fori_loop(0, n, step, 0)

    each(STEPS, lambda s: load_g(s).start())
    load_gate.start()
    load_up.start()
    each(STEPS, lambda s: load_w(s).start())

    barrier = pltpu.get_barrier_semaphore()
    for device in (to_yp, to_ym, to_z, to_zc, to_core, to_zh, to_x(1), to_x(2), to_x(3)):
        pl.semaphore_signal(barrier, inc=1, device_id=device, device_id_type=MESH)
    pl.semaphore_wait(barrier, 9)

    def remote(src, dst, send, recv, device):
        return pltpu.make_async_remote_copy(
            src_ref=src, dst_ref=dst, send_sem=send, recv_sem=recv,
            device_id=device, device_id_type=MESH,
        )

    ROW_ALL, ROW_A, ROW_B, ROW_C = pl.ds(0, ROWS), pl.ds(0, RA), pl.ds(RA, RB), pl.ds(RAB, RC)
    ROW_AB, ROW_BC = pl.ds(0, RAB), pl.ds(RA, RB + RC)
    COL_ALL, COL_0, COL_1 = pl.ds(0, WIDTH), pl.ds(0, HALF), pl.ds(HALF, HALF)

    gather = (
        (own + y, other + y, ROW_AB, COL_ALL, to_z),
        (own + y, own + ym, ROW_ALL, COL_ALL, to_yp),
        (own + y, own + yp, ROW_ALL, COL_ALL, to_ym),
        (other + y, other + ym, ROW_A, COL_ALL, to_yp),
        (other + y, other + yp, ROW_A, COL_ALL, to_ym),
        (own + yp, own + y2, ROW_ALL, COL_0, to_ym),
        (own + ym, own + y2, ROW_ALL, COL_1, to_yp),
        (own + yp, other + yp, ROW_B, COL_ALL, to_z),
        (own + ym, other + ym, ROW_B, COL_ALL, to_z),
        (other + yp, other + y2, ROW_A, COL_0, to_ym),
        (other + ym, other + y2, ROW_A, COL_1, to_yp),
        (own + y2, other + y2, ROW_B, COL_0, to_z),
        (own + y2, other + y2, ROW_B, COL_1, to_z),
        (own + y, other + y, ROW_C, COL_ALL, to_zc),
        (own + yp, other + yp, ROW_C, COL_ALL, to_zc),
        (own + ym, other + ym, ROW_C, COL_ALL, to_zc),
        (own + y2, other + y2, ROW_C, COL_0, to_zc),
        (own + y2, other + y2, ROW_C, COL_1, to_zc),
    )

    def ag_send(k, s):
        leaves, _, rows, cols, device = gather[k]
        ref = gb.at[s, leaves, rows, cols]
        remote(ref, ref, ag_s.at[s], ag_r.at[GATHER_GROUP[k], s], device).start()

    def arrived(ref, sem):
        remote(ref, ref, sem, sem, to_z).wait_recv()

    def left(ref, sem):
        remote(ref, ref, sem, sem, to_z).wait_send()

    def ag_wait(group, s):
        ref = (
            gb.at[s, 0, ROW_AB, :],
            gb.at[s, pl.ds(0, 2)],
            gb.at[s, pl.ds(0, 2), ROW_A, :],
            gb.at[s, 0],
            gb.at[s, pl.ds(0, 3), pl.ds(0, 112), :],
        )[group]
        arrived(ref, ag_r.at[group, s])

    HEAD_B, TAIL_C, ALL = pl.ds(0, RB), pl.ds(RB, RC), slice(None)
    reduction = (
        (other + yp, ROW_B, COL_ALL, rz1, 0, HEAD_B, to_z),
        (other + ym, ROW_B, COL_ALL, rz1, 1, HEAD_B, to_z),
        (other + y2, ROW_B, COL_ALL, rz1, 2, HEAD_B, to_z),
        (other + y2, ROW_A, COL_0, rho, 0, ALL, to_yp),
        (other + y2, ROW_A, COL_1, rho, 1, ALL, to_ym),
        (own + y2, ROW_ALL, COL_0, rhw, 0, ALL, to_yp),
        (own + y2, ROW_ALL, COL_1, rhw, 1, ALL, to_ym),
        (other + yp, ROW_A, COL_ALL, rfo, 0, ALL, to_yp),
        (other + ym, ROW_A, COL_ALL, rfo, 1, ALL, to_ym),
        (own + yp, ROW_ALL, COL_ALL, rfw, 0, ALL, to_yp),
        (own + ym, ROW_ALL, COL_ALL, rfw, 1, ALL, to_ym),
        (other + y, ROW_AB, COL_ALL, rz2, 0, ROW_AB, to_z),
        (other + yp, ROW_C, COL_ALL, rz1, 0, TAIL_C, to_zc),
        (other + ym, ROW_C, COL_ALL, rz1, 1, TAIL_C, to_zc),
        (other + y2, ROW_C, COL_ALL, rz1, 2, TAIL_C, to_zc),
        (other + y, ROW_C, COL_ALL, rz2, 0, ROW_C, to_zc),
    )

    def rs_send(k, s):
        slot, rows, cols, land, index, part, device = reduction[k]
        remote(
            p.at[s, slot, rows, cols], land.at[s, index, part, :],
            rs_s.at[s], rs_r.at[REDUCE_GROUP[k], s], device,
        ).start()

    def rs_wait(group, s):
        ref = (
            p.at[s, pl.ds(0, 3), ROW_AB, :],
            p.at[s, 0, ROW_A, :],
            p.at[s, 0],
            p.at[s, pl.ds(0, 2), ROW_A, :],
            p.at[s, pl.ds(0, 3)],
        )[group]
        arrived(ref, rs_r.at[group, s])

    def core_copy(s):
        return remote(cs.at[s], cr.at[s], c_s, c_r.at[s], to_core)

    def x_copy(s):
        return remote(ck.at[s], xr.at[s], x_s, x_r, to_x(distance(s)))

    zh_copy = remote(zs, zr, zh_s, zh_r, to_zh)
    swapped = h_v.at[pl.ds(other, 4), ROW_C, :]
    h_swap = remote(swapped, hx, sw_s.at[0], sw_r.at[0], to_zh)
    grad_swap = remote(gs, gr, sw_s.at[1], sw_r.at[1], to_zh)

    def a0(s):
        for k in (0, 1, 2, 13):
            ag_send(k, s)

    def a1(s):
        ag_wait(0, s)
        ag_send(3, s)
        ag_send(4, s)
        ag_wait(1, s)
        for k in (5, 6, 7, 8, 14, 15):
            ag_send(k, s)

    def a2(s):
        ag_wait(2, s)
        ag_send(9, s)
        ag_send(10, s)
        ag_wait(3, s)
        for k in (11, 12, 16, 17):
            ag_send(k, s)

    def a3(s):
        ag_wait(4, s)

        def weight_half(side, dst):
            cols = pl.ds(pl.multiple_of(side * HALF, HALF), HALF)

            def tile(t, carry):
                rows = pl.ds(pl.multiple_of(t * 448, 64), 448)
                block = gb[s, :, :, cols].reshape(8 * ROWS, HALF)
                product = jnp.dot(ht_v[rows, :], block, preferred_element_type=F32)
                dst[s, rows, :] = (product * scale).astype(BF16)
                return carry

            lax.fori_loop(0, 2, tile, 0)

        weight_half(1 - core, cs)
        core_copy(s).start()
        weight_half(core, ck)

        def tile(t, carry):
            rows = pl.ds(t * 4, 4)
            block = gb[s, rows].reshape(512, WIDTH)
            product = lax.dot_general(
                block, w_v[s], (((1,), (1,)), ((), ())), preferred_element_type=F32
            ).reshape(4, ROWS, FF)

            @pl.when(s == 0)
            def _():
                hg[rows] = product

            @pl.when(s > 0)
            def _():
                hg[rows] += product

            return carry

        lax.fori_loop(0, 2, tile, 0)

    def d1(s):
        core_copy(s).wait_recv()
        add_rows(ck.at[s], [cr.at[s]], FF)

        @pl.when(s < 6)
        def _():
            x_copy(s).start()

    def d2a():
        arrived(xr, x_r)

        def tile(t, carry):
            sl = pl.ds(pl.multiple_of(t * 16, 16), 16)
            total = ck[7 - zh, sl, :].astype(F32)
            for k, d in ((0, 2), (1, 2), (4, 1)):
                total += xr[k + (1 - zh) * d, sl, :].astype(F32)
            zs[sl, :] = total.astype(BF16)
            return carry

        lax.fori_loop(0, FF // 16, tile, 0)
        zh_copy.start()

    save_d = pltpu.make_async_copy(gd_v, gd_out, st_d)

    def d2b():
        zh_copy.wait_recv()

        def tile(t, carry):
            sl = pl.ds(pl.multiple_of(t * 16, 16), 16)
            total = ck[6 + zh, sl, :].astype(F32) + zr[sl, :].astype(F32)
            for k, d in ((0, 2), (1, 2), (4, 1)):
                total += xr[k + zh * d, sl, :].astype(F32)
            gd_v[sl, :] = total
            return carry

        lax.fori_loop(0, FF // 16, tile, 0)
        save_d.start()

    def r0(s):
        def tile(t, carry):
            rows = pl.ds(t * 4, 4)
            product = jnp.dot(
                h_v[rows].reshape(512, FF), w_v[s], preferred_element_type=F32
            )
            p[s, rows] = product.astype(BF16).reshape(4, ROWS, WIDTH)
            return carry

        lax.fori_loop(0, 2, tile, 0)
        for k in (0, 12, 1, 13, 2, 14, 3, 4):
            rs_send(k, s)

    def r1(s):
        rs_wait(0, s)
        for k, slot in ((2, own + y2), (0, own + yp), (1, own + ym)):
            add_rows(p.at[s, slot, ROW_BC, :], [rz1.at[s, k]], RB + RC)
            if k == 2:
                rs_send(5, s)
                rs_send(6, s)

    def r2(s):
        rs_wait(1, s)
        add_rows(p.at[s, other + yp, ROW_A, COL_0], [rho.at[s, 0]], RA)
        rs_send(7, s)
        add_rows(p.at[s, other + ym, ROW_A, COL_1], [rho.at[s, 1]], RA)
        rs_send(8, s)
        rs_wait(2, s)
        add_rows(p.at[s, own + yp, ROW_ALL, COL_0], [rhw.at[s, 0]], ROWS)
        rs_send(9, s)
        add_rows(p.at[s, own + ym, ROW_ALL, COL_1], [rhw.at[s, 1]], ROWS)
        rs_send(10, s)

    def r3(s):
        rs_send(15, s)
        rs_wait(3, s)
        add_rows(p.at[s, other + y, ROW_A, :], [rfo.at[s, 0], rfo.at[s, 1]], RA)
        rs_send(11, s)

    def save_f(s):
        return pltpu.make_async_copy(p.at[s, te], f_out.at[:, column(s)], st_f)

    def r4(s):
        rs_wait(4, s)
        add_rows(p.at[s, te], [rfw.at[s, 0], rfw.at[s, 1], rz2.at[s, 0]], ROWS)
        save_f(s).start()

    def save_e(e, which):
        first = jnp.where(e < 2, own, other) + (e % 2) * 2
        rows = pl.ds(pl.multiple_of(first * ROWS, 2 * ROWS), 2 * ROWS)
        src, dst = ((gate_v, gg_out), (up_v, gu_out))[which]
        return pltpu.make_async_copy(src.at[rows, :], dst.at[rows, :], st_e.at[which])

    def e0(e):
        first = jnp.where(e < 2, own, other) + (e % 2) * 2

        def tile(t, carry):
            slot = first + t // 8
            row = pl.multiple_of((t % 8) * 16, 16)
            sl = pl.ds(pl.multiple_of(slot * ROWS + row, 16), 16)
            g = gate_v[sl, :].astype(F32)
            u = up_v[sl, :].astype(F32)
            grad = hg[slot, pl.ds(row, 16), :]
            s = jax.nn.sigmoid(g)
            gate_v[sl, :] = (grad * u * s * (1.0 + g * (1.0 - s))).astype(BF16)
            up_v[sl, :] = (grad * (g * s)).astype(BF16)
            return carry

        lax.fori_loop(0, 16, tile, 0)
        save_e(e, 0).start()
        save_e(e, 1).start()

    def swap_tiles(f):
        def tile(t, carry):
            row = pl.multiple_of((t % 3) * 16, 16)
            f(t // 3, pl.ds(row, 16), pl.ds(RAB + row, 16))
            return carry

        lax.fori_loop(0, 4 * (RC // 16), tile, 0)

    def gx():
        def move(k, part, row):
            gs[k, part, :] = hg[other + k, row, :].astype(BF16)

        swap_tiles(move)
        grad_swap.start()

    def gr_stage():
        grad_swap.wait_recv()

        def move(k, part, row):
            hg[other + k, row, :] = gr[k, part, :].astype(F32)

        swap_tiles(move)

    def hidden_rows(slot, row, count):
        def tile(t, carry):
            start = pl.multiple_of(row + t * 16, 16)
            sl = pl.ds(pl.multiple_of(slot * ROWS + start, 16), 16)
            g = gate_v[sl, :].astype(F32)
            u = up_v[sl, :].astype(F32)
            h_v[slot, pl.ds(start, 16), :] = (g * jax.nn.sigmoid(g) * u).astype(BF16)
            return carry

        lax.fori_loop(0, count // 16, tile, 0)

    def hx_stage():
        pltpu.make_async_copy(w_v, w_v, ld_w).wait()
        h_swap.wait_send()
        h_swap.wait_recv()

        def move(k, part, row):
            h_v[other + k, row, :] = hx[k, part, :]

        swap_tiles(move)

        def transpose_tile(t, carry):
            ht_v[:, pl.ds(pl.multiple_of(t * ROWS, ROWS), ROWS)] = h_v[t].T
            return carry

        lax.fori_loop(0, 8, transpose_tile, 0)

    pltpu.make_async_copy(gb.at[:, te], gb.at[:, te], ld_g).wait()
    each(LOOKAHEAD, a0)
    load_gate.wait()
    load_up.wait()

    each(4, lambda k: hidden_rows(other + k, RAB, RC))
    h_swap.start()
    each(4, lambda k: hidden_rows(own + k, 0, ROWS))
    each(4, lambda k: hidden_rows(other + k, 0, RAB))

    def iteration(i, carry):
        def stage(name, f, count=STEPS):
            s = i - OFF[name]

            @pl.when((s >= 0) & (s < count))
            def _():
                f(s)

        stage("A1", a1)
        stage("A2", a2)

        @pl.when(i + LOOKAHEAD < STEPS)
        def _():
            a0(i + LOOKAHEAD)

        stage("HX", lambda s: hx_stage(), 1)
        stage("R0", r0)
        stage("R1", r1)
        stage("R2", r2)
        stage("R3", r3)
        stage("A3", a3)
        stage("GX", lambda s: gx(), 1)
        stage("D1", d1)
        stage("D2A", lambda s: d2a(), 1)
        stage("R4", r4)
        stage("GR", lambda s: gr_stage(), 1)
        stage("E", e0, 4)
        stage("D2B", lambda s: d2b(), 1)
        return carry

    lax.fori_loop(0, ITERS, iteration, 0)

    def finish(s):
        left(gb.at[s, pl.ds(0, 7)], ag_s.at[s])
        left(p.at[s, pl.ds(0, 7)], rs_s.at[s])

    each(STEPS, finish)
    left(cs, c_s)
    left(xr, x_s)
    zh_copy.wait_send()
    grad_swap.wait_send()
    pltpu.make_async_copy(p.at[:, te], p.at[:, te], st_f).wait()
    pltpu.make_async_copy(gate_v, gg_out, st_e.at[0]).wait()
    pltpu.make_async_copy(up_v, gu_out, st_e.at[1]).wait()
    save_d.wait()


PIECES = 2


def settle_kernel(a0, a1, a2, a3, b0, b1, b2, b3, v0, v1, v2, v3, load_sem, save_sem):
    pieces = []
    for k, (src, mid, dst) in enumerate(((a1, v1, b1), (a2, v2, b2), (a0, v0, b0), (a3, v3, b3))):
        count = src.shape[0] // PIECES
        for part in range(PIECES):
            rows = pl.ds(part * count, count)
            n = k * PIECES + part
            pieces.append((
                pltpu.make_async_copy(src.at[rows, :], mid.at[rows, :], load_sem.at[n]),
                pltpu.make_async_copy(mid.at[rows, :], dst.at[rows, :], save_sem.at[n]),
            ))
    for load, _ in pieces:
        load.start()
    for load, save in pieces:
        load.wait()
        save.start()
    for _, save in pieces:
        save.wait()


def settle(outs):
    anywhere = pl.BlockSpec(memory_space=pl.ANY)
    return pl.pallas_call(
        settle_kernel,
        out_shape=tuple(jax.ShapeDtypeStruct(o.shape, o.dtype) for o in outs),
        in_specs=[anywhere] * 4,
        out_specs=[anywhere] * 4,
        scratch_shapes=[pltpu.VMEM(o.shape, o.dtype) for o in outs]
        + [pltpu.SemaphoreType.DMA((4 * PIECES,))] * 2,
        compiler_params=pltpu.CompilerParams(vmem_limit_bytes=60 * 1024 * 1024),
        cost_estimate=pl.CostEstimate(flops=0, bytes_accessed=11_000_000, transcendentals=0),
    )(*outs)


def body(gate_pre, up_pre, down_weight, grad_out):
    replica_rows, ff = gate_pre.shape
    rows, width = grad_out.shape
    scale = 1.0 / math.sqrt(replica_rows * lax.axis_size("dp"))
    vmem, dma = pltpu.VMEM, pltpu.SemaphoreType.DMA
    anywhere = pl.BlockSpec(memory_space=pl.ANY)
    outs = pl.pallas_call(
        functools.partial(kernel, scale),
        out_shape=(
            jax.ShapeDtypeStruct((rows, width), BF16),
            jax.ShapeDtypeStruct((replica_rows, ff), BF16),
            jax.ShapeDtypeStruct((replica_rows, ff), BF16),
            jax.ShapeDtypeStruct((ff, width // 16), F32),
        ),
        in_specs=[anywhere] * 4,
        out_specs=[anywhere] * 4,
        scratch_shapes=[
            vmem((replica_rows, ff), BF16),
            vmem((replica_rows, ff), BF16),
            vmem((STEPS, ff, WIDTH), BF16),
            vmem((8, ROWS, ff), BF16),
            vmem((ff, replica_rows), BF16),
            vmem((STEPS, 8, ROWS, WIDTH), BF16),
            vmem((STEPS, 8, ROWS, WIDTH), BF16),
            vmem((8, ROWS, ff), F32),
            vmem((STEPS, 3, RB + RC, WIDTH), BF16),
            vmem((STEPS, 2, RA, HALF), BF16),
            vmem((STEPS, 2, ROWS, HALF), BF16),
            vmem((STEPS, 2, RA, WIDTH), BF16),
            vmem((STEPS, 2, ROWS, WIDTH), BF16),
            vmem((STEPS, 1, ROWS, WIDTH), BF16),
            vmem((4, RC, ff), BF16),
            vmem((4, RC, ff), BF16),
            vmem((4, RC, ff), BF16),
            vmem((STEPS, ff, HALF), BF16),
            vmem((STEPS, ff, HALF), BF16),
            vmem((STEPS, ff, HALF), BF16),
            vmem((6, ff, HALF), BF16),
            vmem((ff, HALF), BF16),
            vmem((ff, HALF), BF16),
            vmem((ff, HALF), F32),
            dma((STEPS,)), dma((5, STEPS)),
            dma((STEPS,)), dma((5, STEPS)),
            dma, dma((STEPS,)),
            dma, dma,
            dma, dma,
            dma((2,)), dma((2,)),
            dma, dma, dma((2,)),
            dma, dma((2,)), dma,
        ],
        compiler_params=pltpu.CompilerParams(
            collective_id=0, has_side_effects=True, vmem_limit_bytes=60 * 1024 * 1024
        ),
        cost_estimate=pl.CostEstimate(
            flops=6 * replica_rows * ff * width, bytes_accessed=20_000_000, transcendentals=2_000_000
        ),
    )(gate_pre, up_pre, down_weight, grad_out)
    return settle(outs)


def solution(mesh):
    return jax.shard_map(
        body,
        mesh=mesh,
        in_specs=(
            P("dp", "tensor"),
            P("dp", "tensor"),
            P("tensor", None),
            P(("dp", "tensor"), None),
        ),
        out_specs=(
            P(("dp", "tensor"), None),
            P("dp", "tensor"),
            P("dp", "tensor"),
            P("tensor", "dp"),
        ),
        check_vma=False,
    )
```
